32 devices in a mesh: grp: 2 (over y), lib: 4 (over x, core), ptl: 4 (over z).
Axes of the slice: x: 2, y: 2, z: 4, core: 2. Of those that a mesh axis runs over, the one named last changes fastest.
Arguments:
- particles: bfloat16 [1536, 9984], P(('grp', 'lib', 'ptl')), parts along dimension 0
- shifts: int32 [1536], P(('grp', 'lib', 'ptl')), parts along dimension 0, may hold values from 0 to 8
- references: bfloat16 [1024, 9984], P(('grp', 'lib')), parts along dimension 0
- inv_noise: float32 [9984], P('grp'), parts along dimension 0, may hold values from 0.015024038 to 0.060096152
- proj_class: int32 [512], P('lib'), may hold values from 0 to 15
Outputs:
- log_evidence: float32 [1536], P(('grp', 'lib', 'ptl')), parts along dimension 0
- class_posterior: float32 [1536, 16], P(('grp', 'lib', 'ptl')), parts along dimension 0
- weighted_sums: float32 [1024, 9984], P(('grp', 'lib'), 'ptl'), parts along dimension 0
- weight_totals: float32 [1024], P(('grp', 'lib', 'ptl')), parts along dimension 0
The draws below stay inside these ranges and needn't reach their ends.
There are 2 independent parts, one for each index of `grp`. The reference program is written for one: setup_inputs(seed, part) draws one part's arguments, and reference() takes and returns one part's arrays. A program takes and returns all parts, laid end to end along the dimension named above; an argument that names none is the same for every part. Nothing has to cross between parts.
All inputs are finite; a program needn't handle non-finite values.
Results may differ from the reference program's by a relative error of at most 0.0085.
Values may be sent and summed in bfloat16 or wider, within the bound.
A program may use at most 64 MiB of HBM per device.

```python
import math
import jax
import jax.numpy as jnp
from jax import lax

K = 4992
CLASSES = 16
PART_DEV = 48
P_SIZE = 512
N = 768
N_LIB = 4
N_PTL = 4


def ref_field(key):
    signs = jax.random.rademacher(jax.random.fold_in(key, 11), (P_SIZE, 2 * K), jnp.float32)
    magnitude = jax.random.uniform(jax.random.fold_in(key, 13), (P_SIZE, 2 * K), jnp.float32, 0.85, 1.15)
    return signs * magnitude


def shift_field(key):
    return jax.random.randint(jax.random.fold_in(key, 17), (N,), 0, 9, dtype=jnp.int32)


def draw_references(key, part):
    return ref_field(key).astype(jnp.bfloat16)


def draw_shifts(key, part):
    return shift_field(key)


def draw_particles(key, part):
    target = 0.35 * jnp.clip(jax.random.normal(jax.random.fold_in(key, 23), (N, 2 * K), jnp.float32), -5.0, 5.0)
    shift_ids = shift_field(key)
    freq_index = jnp.arange(K, dtype=jnp.int32)
    freq_x = (freq_index % 64).astype(jnp.float32)
    freq_y = (freq_index // 64).astype(jnp.float32)
    step_x = (shift_ids % 3 - 1).astype(jnp.float32)
    step_y = (shift_ids // 3 - 1).astype(jnp.float32)
    angle = (step_x[:, None] * freq_x[None, :] + step_y[:, None] * freq_y[None, :]) * (2.0 * math.pi / 128.0)
    cosine = jnp.cos(angle)
    sine = jnp.sin(angle)
    real_part = target[:, :K]
    imag_part = target[:, K:]
    return jnp.concatenate([real_part * cosine - imag_part * sine, real_part * sine + imag_part * cosine], axis=1).astype(jnp.bfloat16)


def with_ends(entries, key, low, high):
    longest = entries.shape.index(max(entries.shape))
    spots = []
    for shift in (0, 1):
        where = [jax.random.randint(jax.random.fold_in(key, axis), (), 0, length) for axis, length in enumerate(entries.shape)]
        where[longest] = (where[longest] + shift) % entries.shape[longest]
        spots.append(tuple(where))
    return entries.at[spots[0]].set(low).at[spots[1]].set(high)


def setup_inputs(seed: int = 0, part: int = 0) -> dict:
    arg_keys = jax.random.split(jax.random.key(seed), 6)
    part_keys = jax.random.split(jax.random.fold_in(arg_keys[5], part), 6)
    particles = draw_particles(jax.random.fold_in(jax.random.fold_in(arg_keys[5], part), 71), part)
    shifts = draw_shifts(jax.random.fold_in(jax.random.fold_in(arg_keys[5], part), 71), part)
    references = draw_references(jax.random.fold_in(jax.random.fold_in(arg_keys[5], part), 71), part)
    inv_noise = jnp.clip(jnp.exp(jax.random.uniform(part_keys[3], (K,), jnp.float32, math.log(0.015024038), math.log(0.060096152))), 0.015024038, 0.060096152)
    proj_class = with_ends(jax.random.randint(arg_keys[4], (P_SIZE,), 0, CLASSES), jax.random.fold_in(arg_keys[4], 1), 0, CLASSES - 1).astype(jnp.int32)
    return {"particles": particles, "shifts": shifts, "references": references, "inv_noise": inv_noise, "proj_class": proj_class}


def shift_images(images, shift_ids):
    half_width = images.shape[1] // 2
    freq_index = jnp.arange(half_width, dtype=jnp.int32)
    freq_x = (freq_index % 64).astype(jnp.float32)
    freq_y = (freq_index // 64).astype(jnp.float32)
    step_x = (shift_ids % 3 - 1).astype(jnp.float32)
    step_y = (shift_ids // 3 - 1).astype(jnp.float32)
    angle = (step_x[:, None] * freq_x[None, :] + step_y[:, None] * freq_y[None, :]) * (2.0 * math.pi / 128.0)
    cosine = jnp.cos(angle)
    sine = jnp.sin(angle)
    real_part = images[:, :half_width].astype(jnp.float32)
    imag_part = images[:, half_width:].astype(jnp.float32)
    return jnp.concatenate([real_part * cosine + imag_part * sine, imag_part * cosine - real_part * sine], axis=1).astype(jnp.bfloat16)


def prepare_refs(references, inv_noise):
    doubled = jnp.concatenate([inv_noise, inv_noise])
    widened = references.astype(jnp.float32)
    weighted = (widened * doubled[None, :]).astype(jnp.bfloat16)
    half_norm = 0.5 * jnp.sum(widened * widened * doubled[None, :], axis=1)
    return weighted, half_norm


def score_rows(rows, weighted, half_norm):
    return lax.dot_general(rows, weighted, (((1,), (1,)), ((), ())), preferred_element_type=jnp.float32) - half_norm[None, :]


def reference(particles, shifts, references, inv_noise, proj_class):
    shifted = shift_images(particles, shifts)
    weighted, half_norm = prepare_refs(references, inv_noise)
    onehot = (proj_class[:, None] == jnp.arange(CLASSES, dtype=jnp.int32)[None, :]).astype(jnp.bfloat16)
    width = shifted.shape[1]
    grouped = shifted.reshape(N_LIB, N_PTL, PART_DEV, width).transpose(1, 0, 2, 3).reshape(N_PTL, N_LIB * PART_DEV, width)

    def one_group(carry, rows):
        scores = score_rows(rows, weighted, half_norm)
        peak = jnp.max(scores, axis=1)
        evidence = peak + jnp.log(jnp.sum(jnp.exp(scores - peak[:, None]), axis=1))
        post_weights = jnp.exp(scores - evidence[:, None]).astype(jnp.bfloat16)
        shares = jnp.dot(post_weights, onehot, preferred_element_type=jnp.float32)
        sums = lax.dot_general(post_weights, rows, (((0,), (0,)), ((), ())), preferred_element_type=jnp.float32)
        sums = lax.optimization_barrier(sums.astype(jnp.bfloat16)).astype(jnp.float32)
        totals = jnp.sum(post_weights.astype(jnp.float32), axis=0)
        totals = lax.optimization_barrier(totals.astype(jnp.bfloat16)).astype(jnp.float32)
        return (carry[0] + sums, carry[1] + totals), (evidence, shares)

    start = (jnp.zeros((weighted.shape[0], width), jnp.float32), jnp.zeros((weighted.shape[0],), jnp.float32))
    (sums, totals), (evidence, shares) = lax.scan(one_group, start, grouped)
    evidence = evidence.reshape(N_PTL, N_LIB, PART_DEV).transpose(1, 0, 2).reshape(-1)
    shares = shares.reshape(N_PTL, N_LIB, PART_DEV, CLASSES).transpose(1, 0, 2, 3).reshape(-1, CLASSES)
    return (evidence, shares, sums, totals)
```

```python
import functools
import math

import jax
import jax.numpy as jnp
import numpy as np
from jax import lax
from jax.experimental import pallas as pl
from jax.experimental.pallas import tpu as pltpu
from jax.sharding import PartitionSpec as P

CLASSES = 16
LANES = 128
ROWS = 16
LAG = 3
NEAR_AT = 0.5
TOTAL_AT = 2.0
AGG_AT = 2.0
POST_AT = 1.2


def run_loop(low, high, body):
    if high - low <= 4:
        for index in range(low, high):
            body(index)
    else:

        def step(index, carry):
            body(index)
            return carry

        lax.fori_loop(low, high, step, 0)


def diagonal(count):
    shape = (count, count)
    return lax.broadcasted_iota(jnp.int32, shape, 0) == lax.broadcasted_iota(jnp.int32, shape, 1)


def to_column(row):
    return jnp.sum(jnp.where(diagonal(row.shape[1]), row, 0.0), axis=1, keepdims=True)


def to_row(column):
    return jnp.sum(jnp.where(diagonal(column.shape[0]), column, 0.0), axis=0, keepdims=True)


def pair_tile(pair, part_cols, half, span):
    return jnp.minimum((pair * part_cols) // LANES, (half - span) // LANES)


def make_events(n_half, n_first, n_pieces):
    first, last = range(n_first), range(n_first, n_pieces)
    events = [("m", 0, p) for p in first]
    fill = [(kind, 0, p) for p in last for kind in ("m", "x")]
    early = len(fill) // 2
    events += fill[:early]
    for p in first:
        for k in range(n_half):
            events += [("m", k, p)] if k else []
            events += [("m", n_half + k, p)]
    events += fill[early:]
    events += [(kind, k, p) for p in last for k in range(1, n_half) for kind in ("m", "x")]
    return events + [("m", n_half + k, p) for p in last for k in range(n_half)]


def make_sends(n_half, n_first, n_pieces):
    first, last = range(n_first), range(n_first, n_pieces)
    sends = []
    for p in first:
        for k in range(n_half):
            sends += [("m", k, p)] if k else []
            sends += [("m", n_half + k, p)]
    near = [(kind, k, p) for p in last for k in range(1, n_half) for kind in ("m", "x")]
    far = [("m", n_half + k, p) for p in last for k in range(n_half)]
    while near or far:
        sends += near[:2] + far[:1]
        near, far = near[2:], far[1:]
    return sends


def make_steps(events, n_half, n_first, n_pieces):
    number = {event: index for index, event in enumerate(events)}
    steps = [(index, "relay", event) for index, event in enumerate(events)]
    steps += [(index + 0.1, "take", event) for index, event in enumerate(events[LAG:])]
    for p in range(n_pieces):
        kinds = ("m",) if p < n_first else ("m", "x")
        need = max(number[(kind, k, p)] for kind in kinds for k in range(n_half))
        steps.append((need + NEAR_AT, "near", p))
        total = need + NEAR_AT + TOTAL_AT
        if p < n_first:
            need = max(number[("m", n_half + k, p)] for k in range(n_half))
            steps.append((need + NEAR_AT, "far", p))
            steps.append((need + NEAR_AT + AGG_AT, "agg", p))
            total = max(total, need + NEAR_AT + AGG_AT + TOTAL_AT + 0.2)
        steps.append((total, "total", p))
        steps.append((total + POST_AT, "post", p))
    steps.sort(key=lambda step: step[0])
    return [step[1:] for step in steps]


def kernel(
    n_lib,
    n_ptl,
    span,
    n_first,
    part_hbm,
    shift_hbm,
    table_hbm,
    refs_hbm,
    noise_hbm,
    class_hbm,
    gath,
    post,
    small_ref,
    shift_ref,
    table_ref,
    noise_ref,
    class_ref,
    part_ref,
    shifted,
    extra,
    refbuf,
    weighted,
    noise_row,
    near_part,
    near_recv,
    far_part,
    far_recv,
    agg_recv,
    stat,
    in_sem,
    part_sem,
    ref_sem,
    own_sem,
    z_send,
    z_recv,
    x_send,
    x_recv,
    c_send,
    c_recv,
    n_send,
    n_recv,
    f_send,
    f_recv,
    g_send,
    g_recv,
    t_send,
    t_recv,
    p_send,
    p_recv,
):
    lib = lax.axis_index("lib")
    ptl = lax.axis_index("ptl")
    n_x = n_lib // 2
    n_half = n_ptl // 2
    x, core = lib // 2, lib % 2
    mate = 2 * x + 1 - core
    local = lax.rem(ptl, n_half)
    side = ptl // n_half
    n_pieces, _, width = part_ref.shape
    half = width // 2
    part_cols = width // n_ptl
    n_last = n_pieces - n_first
    group = n_lib * ROWS
    tiles = span // LANES

    def near_to(k):
        return side * n_half + lax.rem(local + k, n_half)

    def near_from(k):
        return side * n_half + lax.rem(local + n_half - k, n_half)

    def far_to(k):
        return (1 - side) * n_half + lax.rem(local + k, n_half)

    def far_from(k):
        return (1 - side) * n_half + lax.rem(local + n_half - k, n_half)

    in_copies = [
        pltpu.make_async_copy(source, target, in_sem.at[i])
        for i, (source, target) in enumerate(
            (
                (shift_hbm, shift_ref),
                (table_hbm, table_ref),
                (noise_hbm, noise_ref),
                (class_hbm, class_ref),
            )
        )
    ]
    for copy in in_copies:
        copy.start()
    part_copies = [
        pltpu.make_async_copy(part_hbm.at[pl.ds(p * ROWS, ROWS)], part_ref.at[p], part_sem.at[p])
        for p in range(n_pieces)
    ]
    for copy in part_copies:
        copy.start()
    barrier = pltpu.get_barrier_semaphore()

    def greet_ptl(step):
        pl.semaphore_signal(barrier, inc=1, device_id={"ptl": lax.rem(ptl + step, n_ptl)})

    def greet_lib(step):
        pl.semaphore_signal(barrier, inc=1, device_id={"lib": lax.rem(lib + step, n_lib)})

    run_loop(1, n_ptl, greet_ptl)
    run_loop(1, n_lib, greet_lib)

    own_tile = pair_tile(local, part_cols, half, span)

    def chunk_at(tile):
        return pl.ds(pl.multiple_of(tile * LANES, LANES), span)

    side_tiles = (half // LANES) * side
    ref_copies = [
        pltpu.make_async_copy(
            refs_hbm.at[:, chunk_at(own_tile + (side_tiles if b == 0 else half // LANES - side_tiles))],
            refbuf.at[b],
            ref_sem.at[b],
        )
        for b in range(2)
    ]
    for copy in ref_copies:
        copy.start()

    in_copies[0].wait()
    in_copies[1].wait()
    ids = to_column(shift_ref[...].astype(jnp.float32)).astype(jnp.int32)
    step_y = (ids >= 3).astype(jnp.int32) + (ids >= 6).astype(jnp.int32)
    step_x = (ids - 3 * step_y - 1).astype(jnp.float32)
    step_y = (step_y - 1).astype(jnp.float32)
    cos_x = jnp.where(step_x == 0.0, 1.0, table_ref[0:1, 0:LANES])
    sin_x = step_x * table_ref[1:2, 0:LANES]

    def shift(k, p):
        first = pair_tile(lax.rem(local + k, n_half), part_cols, half, span)
        rows = slice(p * ROWS, (p + 1) * ROWS)
        zero_y, turn_y = step_y[rows] == 0.0, step_y[rows]
        cx, sx = cos_x[rows], sin_x[rows]
        for tile in range(tiles):
            at = pl.multiple_of((first + tile) * LANES, LANES)
            lo, hi = pl.ds(at, LANES), pl.ds(pl.multiple_of(at + half, LANES), LANES)
            cos_y = jnp.where(zero_y, 1.0, table_ref[2:3, lo])
            sin_y = turn_y * table_ref[3:4, lo]
            cosine = cx * cos_y - sx * sin_y
            sine = sx * cos_y + cx * sin_y
            real = part_ref[p, :, lo].astype(jnp.float32)
            imag = part_ref[p, :, hi].astype(jnp.float32)
            to = slice(tile * LANES, (tile + 1) * LANES)
            shifted[k, 0, p, :, to] = (real * cosine + imag * sine).astype(jnp.bfloat16)
            shifted[k, 1, p, :, to] = (imag * cosine - real * sine).astype(jnp.bfloat16)

    events = make_events(n_half, n_first, n_pieces)
    number = {event: index for index, event in enumerate(events)}

    def place(event, source):
        kind, slot, p = event
        return gath.at[p, slot, source] if kind == "m" else extra.at[p - n_first, slot, source]

    def which(event):
        kind, slot, _ = event
        return side if (kind == "m") == (slot < n_half) else 1 - side

    def z_copy(event, back=False):
        kind, slot, p = event
        k = slot % n_half
        target = (near_from(k) if back else near_to(k)) if slot < n_half else (
            far_from(k) if back else far_to(k)
        )
        return pltpu.make_async_remote_copy(
            src_ref=shifted.at[k, which(event), p],
            dst_ref=place(event, lib),
            send_sem=z_send.at[number[event]],
            recv_sem=z_recv.at[number[event]],
            device_id={"ptl": target},
        )

    def x_source(d):
        return lax.rem(x - d + n_x, n_x) * 2 + core

    def lib_copy(event, d, source, send, recv, to):
        here = source is lib and event[1] == 0
        return pltpu.make_async_remote_copy(
            src_ref=shifted.at[0, which(event), event[2]] if here else place(event, source),
            dst_ref=place(event, source),
            send_sem=send.at[number[event], d],
            recv_sem=recv.at[number[event], d],
            device_id={"lib": to},
        )

    def x_copy(event, d):
        return lib_copy(event, d - 1, lib, x_send, x_recv, lax.rem(x + d, n_x) * 2 + core)

    def x_arrival(event, d):
        return lib_copy(event, d - 1, x_source(d), x_send, x_recv, x_source(d))

    def core_copy(event, d):
        return lib_copy(event, d, lib if isinstance(d, int) and d == 0 else x_source(d), c_send, c_recv, mate)

    def core_arrival(event, d):
        return lib_copy(event, d, x_source(d) + 1 - 2 * core, c_send, c_recv, mate)

    def spread(event):
        run_loop(1, n_x, lambda d: x_copy(event, d).start())
        core_copy(event, 0).start()

    def take(event):
        if event[1]:
            z_copy(event, True).wait_recv()
        spread(event)

    def relay(event):
        def forward(d):
            x_arrival(event, d).wait_recv()
            core_copy(event, d).start()

        run_loop(1, n_x, forward)

    def settle(event):
        run_loop(0, n_x, lambda d: core_arrival(event, d).wait_recv())

    own_copies = {}

    def keep(event):
        own_copies[event] = pltpu.make_async_copy(
            shifted.at[0, which(event), event[2]], place(event, lib), own_sem.at[number[event]]
        )
        own_copies[event].start()

    ready, queue = set(), make_sends(n_half, n_first, n_pieces)
    taken = events[:LAG]

    def issue():
        while queue and (queue[0][1] % n_half, queue[0][2]) in ready:
            z_copy(queue.pop(0)).start()
        while taken and (0, taken[0][2]) in ready:
            take(taken.pop(0))

    for p in range(n_pieces):
        part_copies[p].wait()
        for k in range(n_half):
            shift(k, p)
            if not ready:
                pl.semaphore_wait(barrier, n_ptl - 1 + n_lib - 1)
            ready.add((k, p))
            issue()
        keep(("m", 0, p))
        if p >= n_first:
            keep(("x", 0, p))

    in_copies[2].wait()
    in_copies[3].wait()
    for tile in range(half // LANES):
        noise_row[:, tile * LANES : (tile + 1) * LANES] = noise_ref[tile : tile + 1, :]
    offset = local * part_cols - own_tile * LANES
    spot = lax.broadcasted_iota(jnp.int32, (1, span), 1)
    inside = (spot >= offset) & (spot < offset + part_cols)
    noise = jnp.where(inside, noise_row[:, chunk_at(own_tile)], 0.0)
    norms = []
    for b in range(2):
        ref_copies[b].wait()
        widened = refbuf[b].astype(jnp.float32)
        scaled = widened * noise
        weighted[b] = scaled.astype(jnp.bfloat16)
        norms.append(to_row(0.5 * jnp.sum(widened * scaled, axis=1, keepdims=True)))

    def dot(images, b):
        return lax.dot_general(
            images, weighted[b], (((1,), (1,)), ((), ())), preferred_element_type=jnp.float32
        )

    def images_of(ref, low):
        return ref[low : low + n_half].reshape(n_half * group, span)

    def near_copy(p, k, back=False):
        return pltpu.make_async_remote_copy(
            src_ref=near_part.at[p, k],
            dst_ref=near_recv.at[p, k - 1],
            send_sem=n_send.at[p, k - 1],
            recv_sem=n_recv.at[p, k - 1],
            device_id={"ptl": near_to(k) if back else near_from(k)},
        )

    def far_copy(p, k, back=False):
        return pltpu.make_async_remote_copy(
            src_ref=far_part.at[p, k],
            dst_ref=far_recv.at[p, k - 1],
            send_sem=f_send.at[p, k - 1],
            recv_sem=f_recv.at[p, k - 1],
            device_id={"ptl": near_to(k) if back else near_from(k)},
        )

    def agg_copy(p):
        return pltpu.make_async_remote_copy(
            src_ref=far_part.at[p, 0],
            dst_ref=agg_recv.at[p],
            send_sem=g_send.at[p],
            recv_sem=g_recv.at[p],
            device_id={"ptl": far_to(0)},
        )

    def stat_copy(p, d):
        return pltpu.make_async_remote_copy(
            src_ref=stat.at[p, 0],
            dst_ref=stat.at[p, d],
            send_sem=t_send.at[p, d - 1],
            recv_sem=t_recv.at[p, d - 1],
            device_id={"lib": lax.rem(lib + d, n_lib)},
        )

    def post_copy(p, slot, back=False):
        k = slot % n_half
        if slot < n_half:
            target = near_from(k) if back else near_to(k)
        else:
            target = far_from(k) if back else far_to(k)
        return pltpu.make_async_remote_copy(
            src_ref=post.at[p, 0],
            dst_ref=post.at[p, slot],
            send_sem=p_send.at[p, slot - 1],
            recv_sem=p_recv.at[p, slot - 1],
            device_id={"ptl": target},
        )

    onehot = (
        class_ref[...] == lax.broadcasted_iota(jnp.int32, (CLASSES, class_ref.shape[1]), 0)
    ).astype(jnp.bfloat16)
    held = {}

    def step_near(p):
        kinds = ("m",) if p < n_first else ("m", "x")
        for kind in kinds:
            own_copies[(kind, 0, p)].wait()
            for k in range(n_half):
                settle((kind, k, p))
        scores = dot(images_of(gath.at[p], 0), 0) - norms[0]
        if p >= n_first:
            scores = scores + (dot(images_of(extra.at[p - n_first], 0), 1) - norms[1])
        near_part[p] = scores.reshape(n_half, group, -1)
        for k in range(1, n_half):
            near_copy(p, k).start()

    def step_far(p):
        for k in range(n_half):
            settle(("m", n_half + k, p))
        scores = dot(images_of(gath.at[p], n_half), 0) - norms[0]
        far_part[p] = scores.reshape(n_half, group, -1)
        for k in range(1, n_half):
            far_copy(p, k).start()

    def step_agg(p):
        for k in range(1, n_half):
            far_copy(p, k, True).wait_recv()
            far_part[p, 0] = far_part[p, 0] + far_recv[p, k - 1]
        agg_copy(p).start()

    def step_total(p):
        scores = near_part[p, 0]
        for k in range(1, n_half):
            near_copy(p, k, True).wait_recv()
            scores = scores + near_recv[p, k - 1]
        if p < n_first:
            agg_copy(p).wait_recv()
            scores = scores + agg_recv[p]
        scores = scores.T
        peak = jnp.max(scores, axis=0, keepdims=True)
        weights = jnp.exp(scores - peak)
        stat[p, 0, 0:1] = peak
        stat[p, 0, 1:2] = jnp.sum(weights, axis=0, keepdims=True)
        stat[p, 0, 8 : 8 + CLASSES] = jnp.dot(
            onehot, weights.astype(jnp.bfloat16), preferred_element_type=jnp.float32
        )
        run_loop(1, n_lib, lambda d: stat_copy(p, d).start())
        held[p] = weights

    def step_post(p):
        run_loop(1, n_lib, lambda d: stat_copy(p, d).wait_recv())
        peak = stat[p, 0, 0:1]
        top = peak
        for d in range(1, n_lib):
            top = jnp.maximum(top, stat[p, d, 0:1])
        total = jnp.zeros_like(top)
        for d in range(n_lib):
            total = total + stat[p, d, 1:2] * jnp.exp(stat[p, d, 0:1] - top)
        evidence = top + jnp.log(total)
        weights = held.pop(p) * jnp.exp(peak - evidence)
        post[p, 0] = weights.T.astype(jnp.bfloat16)
        for slot in reversed(range(1, n_ptl)):
            post_copy(p, slot).start()
        shares = jnp.zeros((CLASSES, group), jnp.float32)
        for d in range(n_lib):
            shares = shares + stat[p, d, 8 : 8 + CLASSES] * jnp.exp(stat[p, d, 0:1] - evidence)
        mine = slice(p * ROWS, (p + 1) * ROWS)
        for row, values in ((0, evidence), (8, shares)):
            pick = values[:, 0:ROWS]
            for l in range(1, n_lib):
                pick = jnp.where(lib == l, values[:, l * ROWS : (l + 1) * ROWS], pick)
            small_ref[row : row + values.shape[0], mine] = pick

    acts = {
        "relay": relay,
        "take": take,
        "near": step_near,
        "far": step_far,
        "agg": step_agg,
        "total": step_total,
        "post": step_post,
    }
    for name, subject in make_steps(events, n_half, n_first, n_pieces):
        acts[name](subject)

    for p in range(n_pieces):
        for slot in range(1, n_ptl):
            post_copy(p, slot, True).wait_recv()
    for event in events:
        if event[1] >= n_half and event[2] >= n_first:
            settle(event)

    for event in events:
        if event[1]:
            z_copy(event).wait_send()
        run_loop(1, n_x, lambda d: x_copy(event, d).wait_send())
        run_loop(0, n_x, lambda d: core_copy(event, d).wait_send())
    for p in range(n_pieces):
        for k in range(1, n_half):
            near_copy(p, k).wait_send()
            if p < n_first:
                far_copy(p, k).wait_send()
        if p < n_first:
            agg_copy(p).wait_send()
        run_loop(1, n_lib, lambda d: stat_copy(p, d).wait_send())
        for slot in range(1, n_ptl):
            post_copy(p, slot).wait_send()


def finish(n_ptl, blocks, images, weights, small, sums, evid, share, total, buffer, sem):
    part_cols = sums.shape[0]
    span = images.shape[1]
    half = n_ptl * part_cols // 2
    z = lax.axis_index("ptl")
    pair = lax.rem(z, n_ptl // 2)
    offset = pair * part_cols - pair_tile(pair, part_cols, half, span) * LANES
    slack = span - part_cols
    block = span // blocks
    copies = []
    for b in range(blocks):
        cols = slice(b * block, (b + 1) * block)
        buffer[cols] = lax.dot_general(
            weights[...], images[:, cols], (((0,), (0,)), ((), ())), preferred_element_type=jnp.float32
        ).T
        low = b * block - slack if b else 0
        size = (b + 1) * block - slack - low
        copies.append(
            pltpu.make_async_copy(
                buffer.at[pl.ds(pl.multiple_of(offset + low, 8), size)],
                sums.at[pl.ds(low, size)],
                sem.at[b],
            )
        )
        copies[b].start()
    evid[...] = small[0:1]
    share[...] = small[8 : 8 + CLASSES]
    ones = jnp.ones((8, weights.shape[0]), jnp.bfloat16)
    totals = jnp.dot(ones, weights[...], preferred_element_type=jnp.float32)
    count = total.shape[1]
    own_total = totals[0:1, 0:count]
    for y in range(1, n_ptl):
        own_total = jnp.where(z == y, totals[0:1, y * count : (y + 1) * count], own_total)
    total[...] = own_total
    for copy in copies:
        copy.wait()


def trig_table(half):
    index = np.arange(half)
    angle_x = (index % 64) * (2.0 * math.pi / 128.0)
    angle_y = (index // 64) * (2.0 * math.pi / 128.0)
    table = np.zeros((8, half), np.float32)
    table[0], table[1] = np.cos(angle_x), np.sin(angle_x)
    table[2], table[3] = np.cos(angle_y), np.sin(angle_y)
    return table


def on_device(n_lib, n_ptl, particles, shifts, references, inv_noise, proj_class):
    rows, width = particles.shape
    projections = references.shape[0]
    half = width // 2
    part_cols = width // n_ptl
    n_half = n_ptl // 2
    n_x = n_lib // 2
    cover = 0
    for pair in range(n_half):
        cover = max(cover, -(-(pair * part_cols % LANES + part_cols) // LANES))
    span = min(cover * LANES, half)
    n_pieces = rows // ROWS
    n_first = n_pieces // 3
    n_last = n_pieces - n_first
    group = n_lib * ROWS
    own_total = projections // n_ptl
    n_events = len(make_events(n_half, n_first, n_pieces))
    blocks = 5 if (span // LANES) % 5 == 0 else 1
    vmem = pl.BlockSpec(memory_space=pltpu.VMEM)
    far = pl.BlockSpec(memory_space=pltpu.HBM)
    dma = pltpu.SemaphoreType.DMA
    score = (group, projections)
    held_bytes = 2 * n_pieces * n_ptl * group * (span + projections)
    mib = 1024 * 1024
    vmem_limit = (55 - held_bytes // mib) * mib
    images, weights, small = pl.pallas_call(
        functools.partial(kernel, n_lib, n_ptl, span, n_first),
        out_shape=(
            pltpu.VMEM((n_pieces, n_ptl, n_lib, ROWS, span), jnp.bfloat16),
            pltpu.VMEM((n_pieces, n_ptl, group, projections), jnp.bfloat16),
            pltpu.VMEM((8 + CLASSES, rows), jnp.float32),
        ),
        in_specs=[far] * 6,
        out_specs=(vmem, vmem, vmem),
        scratch_shapes=[
            pltpu.VMEM((1, rows), jnp.int32),
            pltpu.VMEM((8, half), jnp.float32),
            pltpu.VMEM((half // LANES, LANES), jnp.float32),
            pltpu.VMEM((1, projections), jnp.int32),
            pltpu.VMEM((n_pieces, ROWS, width), jnp.bfloat16),
            pltpu.VMEM((n_half, 2, n_pieces, ROWS, span), jnp.bfloat16),
            pltpu.VMEM((n_last, n_half, n_lib, ROWS, span), jnp.bfloat16),
            pltpu.VMEM((2, projections, span), jnp.bfloat16),
            pltpu.VMEM((2, projections, span), jnp.bfloat16),
            pltpu.VMEM((1, half), jnp.float32),
            pltpu.VMEM((n_pieces, n_half, *score), jnp.float32),
            pltpu.VMEM((n_pieces, n_half - 1, *score), jnp.float32),
            pltpu.VMEM((n_first, n_half, *score), jnp.float32),
            pltpu.VMEM((n_first, n_half - 1, *score), jnp.float32),
            pltpu.VMEM((n_first, *score), jnp.float32),
            pltpu.VMEM((n_pieces, n_lib, 8 + CLASSES, group), jnp.float32),
            dma((4,)),
            dma((n_pieces,)),
            dma((2,)),
            dma((n_events,)),
            dma((n_events,)),
            dma((n_events,)),
            dma((n_events, n_x - 1)),
            dma((n_events, n_x - 1)),
            dma((n_events, n_x)),
            dma((n_events, n_x)),
            dma((n_pieces, n_half - 1)),
            dma((n_pieces, n_half - 1)),
            dma((n_first, n_half - 1)),
            dma((n_first, n_half - 1)),
            dma((n_first,)),
            dma((n_first,)),
            dma((n_pieces, n_lib - 1)),
            dma((n_pieces, n_lib - 1)),
            dma((n_pieces, n_ptl - 1)),
            dma((n_pieces, n_ptl - 1)),
        ],
        compiler_params=pltpu.CompilerParams(
            collective_id=0, has_side_effects=True, vmem_limit_bytes=vmem_limit
        ),
    )(
        particles,
        shifts[None, :],
        trig_table(half),
        references,
        inv_noise.reshape(-1, LANES),
        proj_class[None, :],
    )
    total_rows = n_pieces * n_ptl * group
    sums, evidence, share, total = pl.pallas_call(
        functools.partial(finish, n_ptl, blocks),
        out_shape=(
            pltpu.HBM((part_cols, projections), jnp.float32),
            jax.ShapeDtypeStruct((1, rows), jnp.float32),
            jax.ShapeDtypeStruct((CLASSES, rows), jnp.float32),
            jax.ShapeDtypeStruct((1, own_total), jnp.float32),
        ),
        in_specs=[vmem, vmem, vmem],
        out_specs=(far, vmem, vmem, vmem),
        scratch_shapes=[pltpu.VMEM((span, projections), jnp.float32), dma((blocks,))],
        compiler_params=pltpu.CompilerParams(vmem_limit_bytes=24 * mib),
    )(images.reshape(total_rows, span), weights.reshape(total_rows, projections), small)
    return evidence[0], share.T, sums.T, total[0]


def solution(mesh):
    in_specs = (
        P(("grp", "lib", "ptl"), None),
        P(("grp", "lib", "ptl")),
        P(("grp", "lib"), None),
        P("grp"),
        P("lib"),
    )
    out_specs = (
        P(("grp", "lib", "ptl")),
        P(("grp", "lib", "ptl"), None),
        P(("grp", "lib"), "ptl"),
        P(("grp", "lib", "ptl")),
    )
    return jax.shard_map(
        functools.partial(on_device, mesh.shape["lib"], mesh.shape["ptl"]),
        mesh=mesh,
        in_specs=in_specs,
        out_specs=out_specs,
        check_vma=False,
    )
```

```python
import functools
import math

import jax
import jax.numpy as jnp
import numpy as np
from jax import lax
from jax.experimental import pallas as pl
from jax.experimental.pallas import tpu as pltpu
from jax.sharding import PartitionSpec as P

CLASSES = 16
LANES = 128
ROWS = 16
LAG = 3
NEAR_AT = 0.5
TOTAL_AT = 1.6
AGG_AT = 2.0
POST_AT = 3.0
HOLD = 0
HOLD_AT = 0.0
EARLY = (5.0, 2.0, 6.0)


def run_loop(low, high, body):
    if high - low <= 4:
        for index in range(low, high):
            body(index)
    else:

        def step(index, carry):
            body(index)
            return carry

        lax.fori_loop(low, high, step, 0)


def diagonal(count):
    shape = (count, count)
    return lax.broadcasted_iota(jnp.int32, shape, 0) == lax.broadcasted_iota(jnp.int32, shape, 1)


def to_column(row):
    return jnp.sum(jnp.where(diagonal(row.shape[1]), row, 0.0), axis=1, keepdims=True)


def to_row(column):
    return jnp.sum(jnp.where(diagonal(column.shape[0]), column, 0.0), axis=0, keepdims=True)


def pair_tile(pair, part_cols, half, span):
    return jnp.minimum((pair * part_cols) // LANES, (half - span) // LANES)


def make_events(n_half, n_first, n_pieces):
    first, last = range(n_first), range(n_first, n_pieces)
    events = [("m", 0, p) for p in first]
    fill = [(kind, 0, p) for p in last for kind in ("m", "x")]
    early = len(fill) // 2
    events += fill[:early]
    for p in first:
        for k in range(n_half):
            events += [("m", k, p)] if k else []
            events += [("m", n_half + k, p)]
    events += fill[early:]
    events += [(kind, k, p) for p in last for k in range(1, n_half) for kind in ("m", "x")]
    return events + [("m", n_half + k, p) for p in last for k in range(n_half)]


def make_sends(n_half, n_first, n_pieces):
    first, last = range(n_first), range(n_first, n_pieces)
    sends = []
    for p in first:
        for k in range(n_half):
            sends += [("m", k, p)] if k else []
            sends += [("m", n_half + k, p)]
    near = [(kind, k, p) for p in last for k in range(1, n_half) for kind in ("m", "x")]
    far = [("m", n_half + k, p) for p in last for k in range(n_half)]
    while near or far:
        sends += near[:2] + far[:1]
        near, far = near[2:], far[1:]
    return sends


def make_steps(events, n_half, n_first, n_pieces):
    number = {event: index for index, event in enumerate(events)}
    steps = [(index, "relay", event) for index, event in enumerate(events)]
    for index, event in enumerate(events[LAG:]):
        late = len(events) - LAG - index <= HOLD
        steps.append((max(index, HOLD_AT if late else 0) + 0.1, "take", event))
    for p in range(n_pieces):
        kinds = ("m",) if p < n_first else ("m", "x")
        need = max(number[(kind, k, p)] for kind in kinds for k in range(n_half))
        steps.append((need + NEAR_AT, "near", p))
        agg_at, total_at, post_at = EARLY if p < n_pieces - 1 else (AGG_AT, TOTAL_AT, POST_AT)
        total = need + NEAR_AT + total_at
        if p < n_first:
            need = max(number[("m", n_half + k, p)] for k in range(n_half))
            steps.append((need + NEAR_AT, "far", p))
            steps.append((need + NEAR_AT + agg_at, "agg", p))
            total = max(total, need + NEAR_AT + agg_at + total_at + 0.2)
        steps.append((total, "total", p))
        steps.append((total + post_at, "post", p))
        if p < n_pieces - 1:
            steps.append((total + post_at + 0.1, "scale", p))
    steps.sort(key=lambda step: step[0])
    return [step[1:] for step in steps]


def kernel(
    n_lib,
    n_ptl,
    span,
    n_first,
    part_hbm,
    shift_hbm,
    table_hbm,
    refs_hbm,
    noise_hbm,
    class_hbm,
    gath,
    final,
    small_ref,
    shift_ref,
    table_ref,
    noise_ref,
    class_ref,
    part_ref,
    shifted,
    extra,
    refbuf,
    weighted,
    noise_row,
    near_part,
    near_recv,
    far_part,
    far_recv,
    agg_recv,
    stat,
    brief,
    post,
    in_sem,
    part_sem,
    ref_sem,
    own_sem,
    z_send,
    z_recv,
    x_send,
    x_recv,
    c_send,
    c_recv,
    n_send,
    n_recv,
    f_send,
    f_recv,
    g_send,
    g_recv,
    t_send,
    t_recv,
    p_send,
    p_recv,
    b_send,
    b_recv,
):
    lib = lax.axis_index("lib")
    ptl = lax.axis_index("ptl")
    n_x = n_lib // 2
    n_half = n_ptl // 2
    x, core = lib // 2, lib % 2
    mate = 2 * x + 1 - core
    local = lax.rem(ptl, n_half)
    side = ptl // n_half
    n_pieces, _, width = part_ref.shape
    half = width // 2
    part_cols = width // n_ptl
    n_last = n_pieces - n_first
    group = n_lib * ROWS
    tiles = span // LANES

    def near_to(k):
        return side * n_half + lax.rem(local + k, n_half)

    def near_from(k):
        return side * n_half + lax.rem(local + n_half - k, n_half)

    def far_to(k):
        return (1 - side) * n_half + lax.rem(local + k, n_half)

    def far_from(k):
        return (1 - side) * n_half + lax.rem(local + n_half - k, n_half)

    in_copies = [
        pltpu.make_async_copy(source, target, in_sem.at[i])
        for i, (source, target) in enumerate(
            (
                (shift_hbm, shift_ref),
                (table_hbm, table_ref),
                (noise_hbm, noise_ref),
                (class_hbm, class_ref),
            )
        )
    ]
    for copy in in_copies:
        copy.start()
    part_copies = [
        pltpu.make_async_copy(part_hbm.at[pl.ds(p * ROWS, ROWS)], part_ref.at[p], part_sem.at[p])
        for p in range(n_pieces)
    ]
    for copy in part_copies:
        copy.start()
    barrier = pltpu.get_barrier_semaphore()

    members = n_ptl * n_lib

    def greet(step):
        other = lax.rem(ptl * n_lib + lib + step, members)
        where = {"ptl": other // n_lib, "lib": lax.rem(other, n_lib)}
        pl.semaphore_signal(barrier, inc=1, device_id=where)

    if members <= 16:
        for step in range(1, members):
            greet(step)
    else:
        run_loop(1, members, greet)

    own_tile = pair_tile(local, part_cols, half, span)

    def chunk_at(tile):
        return pl.ds(pl.multiple_of(tile * LANES, LANES), span)

    side_tiles = (half // LANES) * side
    ref_copies = [
        pltpu.make_async_copy(
            refs_hbm.at[:, chunk_at(own_tile + (side_tiles if b == 0 else half // LANES - side_tiles))],
            refbuf.at[b],
            ref_sem.at[b],
        )
        for b in range(2)
    ]
    for copy in ref_copies:
        copy.start()

    in_copies[0].wait()
    in_copies[1].wait()
    ids = to_column(shift_ref[...].astype(jnp.float32)).astype(jnp.int32)
    step_y = (ids >= 3).astype(jnp.int32) + (ids >= 6).astype(jnp.int32)
    step_x = (ids - 3 * step_y - 1).astype(jnp.float32)
    step_y = (step_y - 1).astype(jnp.float32)
    cos_x = jnp.where(step_x == 0.0, 1.0, table_ref[0:1, 0:LANES])
    sin_x = step_x * table_ref[1:2, 0:LANES]

    def shift(k, p):
        first = pair_tile(lax.rem(local + k, n_half), part_cols, half, span)
        rows = slice(p * ROWS, (p + 1) * ROWS)
        zero_y, turn_y = step_y[rows] == 0.0, step_y[rows]
        cx, sx = cos_x[rows], sin_x[rows]
        for tile in range(tiles):
            at = pl.multiple_of((first + tile) * LANES, LANES)
            lo, hi = pl.ds(at, LANES), pl.ds(pl.multiple_of(at + half, LANES), LANES)
            cos_y = jnp.where(zero_y, 1.0, table_ref[2:3, lo])
            sin_y = turn_y * table_ref[3:4, lo]
            cosine = cx * cos_y - sx * sin_y
            sine = sx * cos_y + cx * sin_y
            real = part_ref[p, :, lo].astype(jnp.float32)
            imag = part_ref[p, :, hi].astype(jnp.float32)
            to = slice(tile * LANES, (tile + 1) * LANES)
            shifted[k, 0, p, :, to] = (real * cosine + imag * sine).astype(jnp.bfloat16)
            shifted[k, 1, p, :, to] = (imag * cosine - real * sine).astype(jnp.bfloat16)

    events = make_events(n_half, n_first, n_pieces)
    number = {event: index for index, event in enumerate(events)}

    def place(event, source):
        kind, slot, p = event
        return gath.at[p, slot, source] if kind == "m" else extra.at[p - n_first, slot, source]

    def which(event):
        kind, slot, _ = event
        return side if (kind == "m") == (slot < n_half) else 1 - side

    def z_copy(event, back=False):
        kind, slot, p = event
        k = slot % n_half
        target = (near_from(k) if back else near_to(k)) if slot < n_half else (
            far_from(k) if back else far_to(k)
        )
        return pltpu.make_async_remote_copy(
            src_ref=shifted.at[k, which(event), p],
            dst_ref=place(event, lib),
            send_sem=z_send.at[number[event]],
            recv_sem=z_recv.at[number[event]],
            device_id={"ptl": target},
        )

    def x_source(d):
        return lax.rem(x - d + n_x, n_x) * 2 + core

    def lib_copy(event, d, source, send, recv, to):
        here = source is lib and event[1] == 0
        return pltpu.make_async_remote_copy(
            src_ref=shifted.at[0, which(event), event[2]] if here else place(event, source),
            dst_ref=place(event, source),
            send_sem=send.at[number[event], d],
            recv_sem=recv.at[number[event], d],
            device_id={"lib": to},
        )

    def x_copy(event, d):
        return lib_copy(event, d - 1, lib, x_send, x_recv, lax.rem(x + d, n_x) * 2 + core)

    def x_arrival(event, d):
        return lib_copy(event, d - 1, x_source(d), x_send, x_recv, x_source(d))

    def core_copy(event, d):
        return lib_copy(event, d, lib if isinstance(d, int) and d == 0 else x_source(d), c_send, c_recv, mate)

    def core_arrival(event, d):
        return lib_copy(event, d, x_source(d) + 1 - 2 * core, c_send, c_recv, mate)

    def spread(event):
        run_loop(1, n_x, lambda d: x_copy(event, d).start())
        core_copy(event, 0).start()

    def take(event):
        if event[1]:
            z_copy(event, True).wait_recv()
        spread(event)

    def relay(event):
        def forward(d):
            x_arrival(event, d).wait_recv()
            core_copy(event, d).start()

        run_loop(1, n_x, forward)

    def settle(event):
        run_loop(0, n_x, lambda d: core_arrival(event, d).wait_recv())

    own_copies = {}

    def keep(event):
        own_copies[event] = pltpu.make_async_copy(
            shifted.at[0, which(event), event[2]], place(event, lib), own_sem.at[number[event]]
        )
        own_copies[event].start()

    ready, queue = set(), make_sends(n_half, n_first, n_pieces)
    taken = events[:LAG]

    def issue():
        while queue and (queue[0][1] % n_half, queue[0][2]) in ready:
            z_copy(queue.pop(0)).start()
        while taken and (0, taken[0][2]) in ready:
            take(taken.pop(0))

    for p in range(n_pieces):
        part_copies[p].wait()
        for k in range(n_half):
            shift(k, p)
            if not ready:
                pl.semaphore_wait(barrier, members - 1)
            ready.add((k, p))
            issue()
        keep(("m", 0, p))
        if p >= n_first:
            keep(("x", 0, p))

    in_copies[2].wait()
    in_copies[3].wait()
    for tile in range(half // LANES):
        noise_row[:, tile * LANES : (tile + 1) * LANES] = noise_ref[tile : tile + 1, :]
    offset = local * part_cols - own_tile * LANES
    spot = lax.broadcasted_iota(jnp.int32, (1, span), 1)
    inside = (spot >= offset) & (spot < offset + part_cols)
    noise = jnp.where(inside, noise_row[:, chunk_at(own_tile)], 0.0)
    norms = []
    for b in range(2):
        ref_copies[b].wait()
        widened = refbuf[b].astype(jnp.float32)
        scaled = widened * noise
        weighted[b] = scaled.astype(jnp.bfloat16)
        norms.append(to_row(0.5 * jnp.sum(widened * scaled, axis=1, keepdims=True)))

    def dot(images, b):
        return lax.dot_general(
            images, weighted[b], (((1,), (1,)), ((), ())), preferred_element_type=jnp.float32
        )

    def images_of(ref, low):
        return ref[low : low + n_half].reshape(n_half * group, span)

    def near_copy(p, k, back=False):
        return pltpu.make_async_remote_copy(
            src_ref=near_part.at[p, k],
            dst_ref=near_recv.at[p, k - 1],
            send_sem=n_send.at[p, k - 1],
            recv_sem=n_recv.at[p, k - 1],
            device_id={"ptl": near_to(k) if back else near_from(k)},
        )

    def far_copy(p, k, back=False):
        return pltpu.make_async_remote_copy(
            src_ref=far_part.at[p, k],
            dst_ref=far_recv.at[p, k - 1],
            send_sem=f_send.at[p, k - 1],
            recv_sem=f_recv.at[p, k - 1],
            device_id={"ptl": near_to(k) if back else near_from(k)},
        )

    def agg_copy(p):
        return pltpu.make_async_remote_copy(
            src_ref=far_part.at[p, 0],
            dst_ref=agg_recv.at[p],
            send_sem=g_send.at[p],
            recv_sem=g_recv.at[p],
            device_id={"ptl": far_to(0)},
        )

    def stat_copy(p, d):
        return pltpu.make_async_remote_copy(
            src_ref=stat.at[p, 0],
            dst_ref=stat.at[p, d],
            send_sem=t_send.at[p, d - 1],
            recv_sem=t_recv.at[p, d - 1],
            device_id={"lib": lax.rem(lib + d, n_lib)},
        )

    def post_copy(p, slot, back=False):
        k = slot % n_half
        if slot < n_half:
            target = near_from(k) if back else near_to(k)
        else:
            target = far_from(k) if back else far_to(k)
        return pltpu.make_async_remote_copy(
            src_ref=post.at[p, 0],
            dst_ref=post.at[p, slot],
            send_sem=p_send.at[p, slot - 1],
            recv_sem=p_recv.at[p, slot - 1],
            device_id={"ptl": target},
        )

    def brief_copy(p, slot, d, back=False):
        k = slot % n_half
        if slot < n_half:
            target = near_from(k) if back else near_to(k)
        else:
            target = far_from(k) if back else far_to(k)
        return pltpu.make_async_remote_copy(
            src_ref=brief.at[p, 0, 0],
            dst_ref=brief.at[p, slot, d],
            send_sem=b_send.at[p, slot - 1, d],
            recv_sem=b_recv.at[p, slot - 1, d],
            device_id={"ptl": target, "lib": lax.rem(lib + (n_lib - d if back else d), n_lib)},
        )

    onehot = (
        class_ref[...] == lax.broadcasted_iota(jnp.int32, (CLASSES, class_ref.shape[1]), 0)
    ).astype(jnp.bfloat16)

    def step_near(p):
        kinds = ("m",) if p < n_first else ("m", "x")
        for kind in kinds:
            own_copies[(kind, 0, p)].wait()
            for k in range(n_half):
                settle((kind, k, p))
        scores = dot(images_of(gath.at[p], 0), 0) - norms[0]
        if p >= n_first:
            scores = scores + (dot(images_of(extra.at[p - n_first], 0), 1) - norms[1])
        near_part[p] = scores.reshape(n_half, group, -1)
        for k in range(1, n_half):
            near_copy(p, k).start()

    def step_far(p):
        for k in range(n_half):
            settle(("m", n_half + k, p))
        scores = dot(images_of(gath.at[p], n_half), 0) - norms[0]
        far_part[p] = scores.reshape(n_half, group, -1)
        for k in range(1, n_half):
            far_copy(p, k).start()

    def step_agg(p):
        for k in range(1, n_half):
            far_copy(p, k, True).wait_recv()
            far_part[p, 0] = far_part[p, 0] + far_recv[p, k - 1]
        agg_copy(p).start()

    def step_total(p):
        scores = near_part[p, 0]
        for k in range(1, n_half):
            near_copy(p, k, True).wait_recv()
            scores = scores + near_recv[p, k - 1]
        if p < n_first:
            agg_copy(p).wait_recv()
            scores = scores + agg_recv[p]
        scores = scores.T
        peak = jnp.max(scores, axis=0, keepdims=True)
        weights = jnp.exp(scores - peak)
        mass = jnp.sum(weights, axis=0, keepdims=True)
        brief[p, 0, 0, 0:1] = peak
        brief[p, 0, 0, 1:2] = mass
        post[p, 0] = weights.T.astype(jnp.bfloat16)
        for slot in reversed(range(1, n_ptl)):
            post_copy(p, slot).start()
            run_loop(0, n_lib, lambda d: brief_copy(p, slot, d).start())
        stat[p, 0, 0:1] = peak
        stat[p, 0, 1:2] = mass
        stat[p, 0, 8 : 8 + CLASSES] = jnp.dot(
            onehot, weights.astype(jnp.bfloat16), preferred_element_type=jnp.float32
        )
        run_loop(1, n_lib, lambda d: stat_copy(p, d).start())

    def step_post(p):
        run_loop(1, n_lib, lambda d: stat_copy(p, d).wait_recv())
        top = stat[p, 0, 0:1]
        for d in range(1, n_lib):
            top = jnp.maximum(top, stat[p, d, 0:1])
            brief[p, 0, d] = stat[p, d, 0:2]
        total = jnp.zeros_like(top)
        for d in range(n_lib):
            total = total + stat[p, d, 1:2] * jnp.exp(stat[p, d, 0:1] - top)
        evidence = top + jnp.log(total)
        shares = jnp.zeros((CLASSES, group), jnp.float32)
        for d in range(n_lib):
            shares = shares + stat[p, d, 8 : 8 + CLASSES] * jnp.exp(stat[p, d, 0:1] - evidence)
        mine = slice(p * ROWS, (p + 1) * ROWS)
        for row, values in ((0, evidence), (8, shares)):
            pick = values[:, 0:ROWS]
            for l in range(1, n_lib):
                pick = jnp.where(lib == l, values[:, l * ROWS : (l + 1) * ROWS], pick)
            small_ref[row : row + values.shape[0], mine] = pick

    def step_scale(p):
        for slot in range(1, n_ptl):
            post_copy(p, slot, True).wait_recv()
            run_loop(0, n_lib, lambda d: brief_copy(p, slot, d, True).wait_recv())
        for slot in range(0, n_ptl, 2):
            scales = []
            for one in (slot, slot + 1):
                top = brief[p, one, 0, 0:1]
                for d in range(1, n_lib):
                    top = jnp.maximum(top, brief[p, one, d, 0:1])
                total = jnp.zeros_like(top)
                for d in range(n_lib):
                    total = total + brief[p, one, d, 1:2] * jnp.exp(brief[p, one, d, 0:1] - top)
                scales.append(jnp.exp(brief[p, one, 0, 0:1] - (top + jnp.log(total))))
            pair = post[p, slot : slot + 2].reshape(2 * group, -1).astype(jnp.float32).T
            low = (p * n_ptl + slot) * group
            final[:, low : low + 2 * group] = (
                pair * jnp.concatenate(scales, axis=1)
            ).astype(jnp.bfloat16)

    acts = {
        "relay": relay,
        "take": take,
        "near": step_near,
        "far": step_far,
        "agg": step_agg,
        "total": step_total,
        "post": step_post,
        "scale": step_scale,
    }
    for name, subject in make_steps(events, n_half, n_first, n_pieces):
        acts[name](subject)

    step_scale(n_pieces - 1)
    for event in events:
        if event[1] >= n_half and event[2] >= n_first:
            settle(event)

    for event in events:
        if event[1]:
            z_copy(event).wait_send()
        run_loop(1, n_x, lambda d: x_copy(event, d).wait_send())
        run_loop(0, n_x, lambda d: core_copy(event, d).wait_send())
    for p in range(n_pieces):
        for k in range(1, n_half):
            near_copy(p, k).wait_send()
            if p < n_first:
                far_copy(p, k).wait_send()
        if p < n_first:
            agg_copy(p).wait_send()
        run_loop(1, n_lib, lambda d: stat_copy(p, d).wait_send())
        for slot in range(1, n_ptl):
            post_copy(p, slot).wait_send()
            run_loop(0, n_lib, lambda d: brief_copy(p, slot, d).wait_send())


def finish(n_ptl, blocks, images, weights, small, sums, evid, share, total, buffer, sem):
    part_cols = sums.shape[0]
    span = images.shape[1]
    half = n_ptl * part_cols // 2
    z = lax.axis_index("ptl")
    pair = lax.rem(z, n_ptl // 2)
    offset = pair * part_cols - pair_tile(pair, part_cols, half, span) * LANES
    slack = span - part_cols
    block = span // blocks
    copies = []
    for b in range(blocks):
        cols = slice(b * block, (b + 1) * block)
        buffer[cols] = jnp.dot(
            weights[...], images[:, cols], preferred_element_type=jnp.float32
        ).T
        low = b * block - slack if b else 0
        size = (b + 1) * block - slack - low
        copies.append(
            pltpu.make_async_copy(
                buffer.at[pl.ds(pl.multiple_of(offset + low, 8), size)],
                sums.at[pl.ds(low, size)],
                sem.at[b],
            )
        )
        copies[b].start()
    evid[...] = small[0:1]
    share[...] = small[8 : 8 + CLASSES]
    ones = jnp.ones((8, weights.shape[1]), jnp.bfloat16)
    totals = lax.dot_general(
        ones, weights[...], (((1,), (1,)), ((), ())), preferred_element_type=jnp.float32
    )
    count = total.shape[1]
    own_total = totals[0:1, 0:count]
    for y in range(1, n_ptl):
        own_total = jnp.where(z == y, totals[0:1, y * count : (y + 1) * count], own_total)
    total[...] = own_total
    for copy in copies:
        copy.wait()


def trig_table(half):
    index = np.arange(half)
    angle_x = (index % 64) * (2.0 * math.pi / 128.0)
    angle_y = (index // 64) * (2.0 * math.pi / 128.0)
    table = np.zeros((8, half), np.float32)
    table[0], table[1] = np.cos(angle_x), np.sin(angle_x)
    table[2], table[3] = np.cos(angle_y), np.sin(angle_y)
    return table


def on_device(n_lib, n_ptl, particles, shifts, references, inv_noise, proj_class):
    rows, width = particles.shape
    projections = references.shape[0]
    half = width // 2
    part_cols = width // n_ptl
    n_half = n_ptl // 2
    n_x = n_lib // 2
    cover = 0
    for pair in range(n_half):
        cover = max(cover, -(-(pair * part_cols % LANES + part_cols) // LANES))
    span = min(cover * LANES, half)
    n_pieces = rows // ROWS
    n_first = 1
    n_last = n_pieces - n_first
    group = n_lib * ROWS
    own_total = projections // n_ptl
    n_events = len(make_events(n_half, n_first, n_pieces))
    blocks = 5 if (span // LANES) % 5 == 0 else 1
    vmem = pl.BlockSpec(memory_space=pltpu.VMEM)
    far = pl.BlockSpec(memory_space=pltpu.HBM)
    dma = pltpu.SemaphoreType.DMA
    score = (group, projections)
    held_bytes = 2 * n_pieces * n_ptl * group * (span + projections)
    mib = 1024 * 1024
    vmem_limit = (55 - held_bytes // mib) * mib
    images, weights, small = pl.pallas_call(
        functools.partial(kernel, n_lib, n_ptl, span, n_first),
        out_shape=(
            pltpu.VMEM((n_pieces, n_ptl, n_lib, ROWS, span), jnp.bfloat16),
            pltpu.VMEM((projections, n_pieces * n_ptl * group), jnp.bfloat16),
            pltpu.VMEM((8 + CLASSES, rows), jnp.float32),
        ),
        in_specs=[far] * 6,
        out_specs=(vmem, vmem, vmem),
        scratch_shapes=[
            pltpu.VMEM((1, rows), jnp.int32),
            pltpu.VMEM((8, half), jnp.float32),
            pltpu.VMEM((half // LANES, LANES), jnp.float32),
            pltpu.VMEM((1, projections), jnp.int32),
            pltpu.VMEM((n_pieces, ROWS, width), jnp.bfloat16),
            pltpu.VMEM((n_half, 2, n_pieces, ROWS, span), jnp.bfloat16),
            pltpu.VMEM((n_last, n_half, n_lib, ROWS, span), jnp.bfloat16),
            pltpu.VMEM((2, projections, span), jnp.bfloat16),
            pltpu.VMEM((2, projections, span), jnp.bfloat16),
            pltpu.VMEM((1, half), jnp.float32),
            pltpu.VMEM((n_pieces, n_half, *score), jnp.float32),
            pltpu.VMEM((n_pieces, n_half - 1, *score), jnp.float32),
            pltpu.VMEM((n_first, n_half, *score), jnp.float32),
            pltpu.VMEM((n_first, n_half - 1, *score), jnp.float32),
            pltpu.VMEM((n_first, *score), jnp.float32),
            pltpu.VMEM((n_pieces, n_lib, 8 + CLASSES, group), jnp.float32),
            pltpu.VMEM((n_pieces, n_ptl, n_lib, 2, group), jnp.float32),
            pltpu.VMEM((n_pieces, n_ptl, group, projections), jnp.bfloat16),
            dma((4,)),
            dma((n_pieces,)),
            dma((2,)),
            dma((n_events,)),
            dma((n_events,)),
            dma((n_events,)),
            dma((n_events, n_x - 1)),
            dma((n_events, n_x - 1)),
            dma((n_events, n_x)),
            dma((n_events, n_x)),
            dma((n_pieces, n_half - 1)),
            dma((n_pieces, n_half - 1)),
            dma((n_first, n_half - 1)),
            dma((n_first, n_half - 1)),
            dma((n_first,)),
            dma((n_first,)),
            dma((n_pieces, n_lib - 1)),
            dma((n_pieces, n_lib - 1)),
            dma((n_pieces, n_ptl - 1)),
            dma((n_pieces, n_ptl - 1)),
            dma((n_pieces, n_ptl - 1, n_lib)),
            dma((n_pieces, n_ptl - 1, n_lib)),
        ],
        compiler_params=pltpu.CompilerParams(
            collective_id=0, has_side_effects=True, vmem_limit_bytes=vmem_limit
        ),
    )(
        particles,
        shifts[None, :],
        trig_table(half),
        references,
        inv_noise.reshape(-1, LANES),
        proj_class[None, :],
    )
    total_rows = n_pieces * n_ptl * group
    sums, evidence, share, total = pl.pallas_call(
        functools.partial(finish, n_ptl, blocks),
        out_shape=(
            pltpu.HBM((part_cols, projections), jnp.float32),
            jax.ShapeDtypeStruct((1, rows), jnp.float32),
            jax.ShapeDtypeStruct((CLASSES, rows), jnp.float32),
            jax.ShapeDtypeStruct((1, own_total), jnp.float32),
        ),
        in_specs=[vmem, vmem, vmem],
        out_specs=(far, vmem, vmem, vmem),
        scratch_shapes=[pltpu.VMEM((span, projections), jnp.float32), dma((blocks,))],
        compiler_params=pltpu.CompilerParams(vmem_limit_bytes=24 * mib),
    )(images.reshape(total_rows, span), weights, small)
    return evidence[0], share.T, sums.T, total[0]


def solution(mesh):
    in_specs = (
        P(("grp", "lib", "ptl"), None),
        P(("grp", "lib", "ptl")),
        P(("grp", "lib"), None),
        P("grp"),
        P("lib"),
    )
    out_specs = (
        P(("grp", "lib", "ptl")),
        P(("grp", "lib", "ptl"), None),
        P(("grp", "lib"), "ptl"),
        P(("grp", "lib", "ptl")),
    )
    return jax.shard_map(
        functools.partial(on_device, mesh.shape["lib"], mesh.shape["ptl"]),
        mesh=mesh,
        in_specs=in_specs,
        out_specs=out_specs,
        check_vma=False,
    )
```

```python
import functools
import math

import jax
import jax.numpy as jnp
import numpy as np
from jax import lax
from jax.experimental import pallas as pl
from jax.experimental.pallas import tpu as pltpu
from jax.sharding import PartitionSpec as P

CLASSES = 16
LANES = 128
ROWS = 16
LAG = 3
AHEAD = (1.0,)
TOTAL_AT = 2.0
EARLY_AT = 2.2
AGG_AT = 5.0
FIRST_AT = 2.2


def run_loop(low, high, body):
    if high - low <= 4:
        for index in range(low, high):
            body(index)
    else:

        def step(index, carry):
            body(index)
            return carry

        lax.fori_loop(low, high, step, 0)


def diagonal(count):
    shape = (count, count)
    return lax.broadcasted_iota(jnp.int32, shape, 0) == lax.broadcasted_iota(jnp.int32, shape, 1)


def to_column(row):
    return jnp.sum(jnp.where(diagonal(row.shape[1]), row, 0.0), axis=1, keepdims=True)


def to_row(column):
    return jnp.sum(jnp.where(diagonal(column.shape[0]), column, 0.0), axis=0, keepdims=True)


def pair_tile(pair, part_cols, half, span):
    return jnp.minimum((pair * part_cols) // LANES, (half - span) // LANES)


def make_events(n_half, n_first, n_pieces):
    first, last = range(n_first), range(n_first, n_pieces)
    events = [("m", 0, p) for p in first]
    fill = [(kind, 0, p) for p in last for kind in ("m", "x")]
    early = len(fill) // 2
    events += fill[:early]
    for p in first:
        for k in range(n_half):
            events += [("m", k, p)] if k else []
            events += [("m", n_half + k, p)]
    events += fill[early:]
    events += [(kind, k, p) for p in last for k in range(1, n_half) for kind in ("m", "x")]
    return events + [("m", n_half + k, p) for p in last for k in range(n_half)]


def make_sends(n_half, n_first, n_pieces):
    first, last = range(n_first), range(n_first, n_pieces)
    sends = []
    for p in first:
        for k in range(n_half):
            sends += [("m", k, p)] if k else []
            sends += [("m", n_half + k, p)]
    near = [(kind, k, p) for p in last for k in range(1, n_half) for kind in ("m", "x")]
    far = [("m", n_half + k, p) for p in last for k in range(n_half)]
    while near or far:
        sends += near[:2] + far[:1]
        near, far = near[2:], far[1:]
    return sends


def make_steps(events, n_half, n_first, n_pieces):
    number = {event: index for index, event in enumerate(events)}
    count = len(events)
    steps = [(index, "relay", event) for index, event in enumerate(events)]
    for index, event in enumerate(events[LAG:]):
        at = index if index + LAG < count - len(AHEAD) else index - AHEAD[index + LAG - count]
        steps.append((at + 0.1, "take", event))
    totals = []
    for p in range(n_pieces):
        kinds = ("m",) if p < n_first else ("m", "x")
        need = max(number[(kind, k, p)] for kind in kinds for k in range(n_half))
        steps.append((need + 0.5, "near", p))
        total = need + 0.5 + (TOTAL_AT if p == n_pieces - 1 else EARLY_AT)
        if p < n_first:
            need = max(number[("m", n_half + k, p)] for k in range(n_half))
            steps.append((need + 0.6, "far", p))
            steps.append((need + 0.6 + AGG_AT, "agg", p))
            total = max(total, need + 0.6 + AGG_AT + FIRST_AT)
        totals.append(total)
    totals[-1] = max(totals[-1], max(totals) + 0.01)
    steps += [(total, "total", p) for p, total in enumerate(totals)]
    steps.sort(key=lambda step: step[0])
    return [step[1:] for step in steps]


def kernel(
    n_lib,
    n_ptl,
    span,
    n_first,
    part_hbm,
    shift_hbm,
    table_hbm,
    refs_hbm,
    noise_hbm,
    class_hbm,
    gath,
    final,
    small_ref,
    shift_ref,
    table_ref,
    noise_ref,
    class_ref,
    part_ref,
    shifted,
    extra,
    refbuf,
    weighted,
    noise_row,
    near_part,
    near_recv,
    far_part,
    far_recv,
    agg_recv,
    share_out,
    share_in,
    factor,
    brief,
    post,
    in_sem,
    part_sem,
    ref_sem,
    own_sem,
    z_send,
    z_recv,
    x_send,
    x_recv,
    c_send,
    c_recv,
    n_send,
    n_recv,
    f_send,
    f_recv,
    g_send,
    g_recv,
    t_send,
    t_recv,
    p_send,
    p_recv,
    b_send,
    b_recv,
):
    lib = lax.axis_index("lib")
    ptl = lax.axis_index("ptl")
    n_x = n_lib // 2
    n_half = n_ptl // 2
    x, core = lib // 2, lib % 2
    mate = 2 * x + 1 - core
    local = lax.rem(ptl, n_half)
    side = ptl // n_half
    n_pieces, _, width = part_ref.shape
    half = width // 2
    part_cols = width // n_ptl
    n_last = n_pieces - n_first
    group = n_lib * ROWS
    tiles = span // LANES

    def near_to(k):
        return side * n_half + lax.rem(local + k, n_half)

    def near_from(k):
        return side * n_half + lax.rem(local + n_half - k, n_half)

    def far_to(k):
        return (1 - side) * n_half + lax.rem(local + k, n_half)

    def far_from(k):
        return (1 - side) * n_half + lax.rem(local + n_half - k, n_half)

    in_copies = [
        pltpu.make_async_copy(source, target, in_sem.at[i])
        for i, (source, target) in enumerate(
            (
                (shift_hbm, shift_ref),
                (table_hbm, table_ref),
                (noise_hbm, noise_ref),
                (class_hbm, class_ref),
            )
        )
    ]
    for copy in in_copies:
        copy.start()
    part_copies = [
        pltpu.make_async_copy(part_hbm.at[pl.ds(p * ROWS, ROWS)], part_ref.at[p], part_sem.at[p])
        for p in range(n_pieces)
    ]
    for copy in part_copies:
        copy.start()
    barrier = pltpu.get_barrier_semaphore()

    def greet_ptl(step):
        pl.semaphore_signal(barrier, inc=1, device_id={"ptl": lax.rem(ptl + step, n_ptl)})

    def greet_lib(step):
        pl.semaphore_signal(barrier, inc=1, device_id={"lib": lax.rem(lib + step, n_lib)})

    run_loop(1, n_ptl, greet_ptl)
    run_loop(1, n_lib, greet_lib)

    own_tile = pair_tile(local, part_cols, half, span)

    def chunk_at(tile):
        return pl.ds(pl.multiple_of(tile * LANES, LANES), span)

    side_tiles = (half // LANES) * side
    ref_copies = [
        pltpu.make_async_copy(
            refs_hbm.at[:, chunk_at(own_tile + (side_tiles if b == 0 else half // LANES - side_tiles))],
            refbuf.at[b],
            ref_sem.at[b],
        )
        for b in range(2)
    ]
    for copy in ref_copies:
        copy.start()

    in_copies[0].wait()
    in_copies[1].wait()
    ids = to_column(shift_ref[...].astype(jnp.float32)).astype(jnp.int32)
    step_y = (ids >= 3).astype(jnp.int32) + (ids >= 6).astype(jnp.int32)
    step_x = (ids - 3 * step_y - 1).astype(jnp.float32)
    step_y = (step_y - 1).astype(jnp.float32)
    cos_x = jnp.where(step_x == 0.0, 1.0, table_ref[0:1, 0:LANES])
    sin_x = step_x * table_ref[1:2, 0:LANES]

    def shift(k, p):
        first = pair_tile(lax.rem(local + k, n_half), part_cols, half, span)
        rows = slice(p * ROWS, (p + 1) * ROWS)
        zero_y, turn_y = step_y[rows] == 0.0, step_y[rows]
        cx, sx = cos_x[rows], sin_x[rows]
        for tile in range(tiles):
            at = pl.multiple_of((first + tile) * LANES, LANES)
            lo, hi = pl.ds(at, LANES), pl.ds(pl.multiple_of(at + half, LANES), LANES)
            cos_y = jnp.where(zero_y, 1.0, table_ref[2:3, lo])
            sin_y = turn_y * table_ref[3:4, lo]
            cosine = cx * cos_y - sx * sin_y
            sine = sx * cos_y + cx * sin_y
            real = part_ref[p, :, lo].astype(jnp.float32)
            imag = part_ref[p, :, hi].astype(jnp.float32)
            to = slice(tile * LANES, (tile + 1) * LANES)
            shifted[k, 0, p, :, to] = (real * cosine + imag * sine).astype(jnp.bfloat16)
            shifted[k, 1, p, :, to] = (imag * cosine - real * sine).astype(jnp.bfloat16)

    events = make_events(n_half, n_first, n_pieces)
    number = {event: index for index, event in enumerate(events)}

    def place(event, source):
        kind, slot, p = event
        return gath.at[p, slot, source] if kind == "m" else extra.at[p - n_first, slot, source]

    def which(event):
        kind, slot, _ = event
        return side if (kind == "m") == (slot < n_half) else 1 - side

    def z_copy(event, back=False):
        kind, slot, p = event
        k = slot % n_half
        target = (near_from(k) if back else near_to(k)) if slot < n_half else (
            far_from(k) if back else far_to(k)
        )
        return pltpu.make_async_remote_copy(
            src_ref=shifted.at[k, which(event), p],
            dst_ref=place(event, lib),
            send_sem=z_send.at[number[event]],
            recv_sem=z_recv.at[number[event]],
            device_id={"ptl": target},
        )

    def x_source(d):
        return lax.rem(x - d + n_x, n_x) * 2 + core

    def lib_copy(event, d, source, send, recv, to):
        here = source is lib and event[1] == 0
        return pltpu.make_async_remote_copy(
            src_ref=shifted.at[0, which(event), event[2]] if here else place(event, source),
            dst_ref=place(event, source),
            send_sem=send.at[number[event], d],
            recv_sem=recv.at[number[event], d],
            device_id={"lib": to},
        )

    def x_copy(event, d):
        return lib_copy(event, d - 1, lib, x_send, x_recv, lax.rem(x + d, n_x) * 2 + core)

    def x_arrival(event, d):
        return lib_copy(event, d - 1, x_source(d), x_send, x_recv, x_source(d))

    def core_copy(event, d):
        return lib_copy(event, d, lib if isinstance(d, int) and d == 0 else x_source(d), c_send, c_recv, mate)

    def core_arrival(event, d):
        return lib_copy(event, d, x_source(d) + 1 - 2 * core, c_send, c_recv, mate)

    def spread(event):
        run_loop(1, n_x, lambda d: x_copy(event, d).start())
        core_copy(event, 0).start()

    def take(event):
        if event[1]:
            z_copy(event, True).wait_recv()
        spread(event)

    def relay(event):
        def forward(d):
            x_arrival(event, d).wait_recv()
            core_copy(event, d).start()

        run_loop(1, n_x, forward)

    def settle(event):
        run_loop(0, n_x, lambda d: core_arrival(event, d).wait_recv())

    own_copies = {}

    def keep(event):
        own_copies[event] = pltpu.make_async_copy(
            shifted.at[0, which(event), event[2]], place(event, lib), own_sem.at[number[event]]
        )
        own_copies[event].start()

    ready, queue = set(), make_sends(n_half, n_first, n_pieces)
    taken = events[:LAG]

    def issue():
        while queue and (queue[0][1] % n_half, queue[0][2]) in ready:
            z_copy(queue.pop(0)).start()
        while taken and (0, taken[0][2]) in ready:
            take(taken.pop(0))

    for p in range(n_pieces):
        part_copies[p].wait()
        for k in range(n_half):
            shift(k, p)
            if not ready:
                pl.semaphore_wait(barrier, n_ptl - 1 + n_lib - 1)
            ready.add((k, p))
            issue()
        keep(("m", 0, p))
        if p >= n_first:
            keep(("x", 0, p))

    in_copies[2].wait()
    in_copies[3].wait()
    for tile in range(half // LANES):
        noise_row[:, tile * LANES : (tile + 1) * LANES] = noise_ref[tile : tile + 1, :]
    offset = local * part_cols - own_tile * LANES
    spot = lax.broadcasted_iota(jnp.int32, (1, span), 1)
    inside = (spot >= offset) & (spot < offset + part_cols)
    noise = jnp.where(inside, noise_row[:, chunk_at(own_tile)], 0.0)
    norms = []
    for b in range(2):
        ref_copies[b].wait()
        widened = refbuf[b].astype(jnp.float32)
        scaled = widened * noise
        weighted[b] = scaled.astype(jnp.bfloat16)
        norms.append(to_row(0.5 * jnp.sum(widened * scaled, axis=1, keepdims=True)))

    def dot(images, b):
        return lax.dot_general(
            images, weighted[b], (((1,), (1,)), ((), ())), preferred_element_type=jnp.float32
        )

    def images_of(ref, low):
        return ref[low : low + n_half].reshape(n_half * group, span)

    def near_copy(p, k, back=False):
        return pltpu.make_async_remote_copy(
            src_ref=near_part.at[p, k],
            dst_ref=near_recv.at[p, k - 1],
            send_sem=n_send.at[p, k - 1],
            recv_sem=n_recv.at[p, k - 1],
            device_id={"ptl": near_to(k) if back else near_from(k)},
        )

    def far_copy(p, k, back=False):
        return pltpu.make_async_remote_copy(
            src_ref=far_part.at[p, k],
            dst_ref=far_recv.at[p, k - 1],
            send_sem=f_send.at[p, k - 1],
            recv_sem=f_recv.at[p, k - 1],
            device_id={"ptl": near_to(k) if back else near_from(k)},
        )

    def agg_copy(p):
        return pltpu.make_async_remote_copy(
            src_ref=far_part.at[p, 0],
            dst_ref=agg_recv.at[p],
            send_sem=g_send.at[p],
            recv_sem=g_recv.at[p],
            device_id={"ptl": far_to(0)},
        )

    def share_copy(d):
        to = lax.rem(lib + d, n_lib)
        return pltpu.make_async_remote_copy(
            src_ref=share_out.at[to],
            dst_ref=share_in.at[d - 1],
            send_sem=t_send.at[d - 1],
            recv_sem=t_recv.at[d - 1],
            device_id={"lib": to},
        )

    def post_copy(p, slot, back=False):
        k = slot % n_half
        if slot < n_half:
            target = near_from(k) if back else near_to(k)
        else:
            target = far_from(k) if back else far_to(k)
        return pltpu.make_async_remote_copy(
            src_ref=post.at[p, 0],
            dst_ref=post.at[p, slot],
            send_sem=p_send.at[p, slot - 1],
            recv_sem=p_recv.at[p, slot - 1],
            device_id={"ptl": target},
        )

    def brief_copy(slot, d, back=False):
        k = slot % n_half
        if slot < n_half:
            target = near_from(k) if back else near_to(k)
        else:
            target = far_from(k) if back else far_to(k)
        return pltpu.make_async_remote_copy(
            src_ref=brief.at[0, 0],
            dst_ref=brief.at[slot, d],
            send_sem=b_send.at[slot, d],
            recv_sem=b_recv.at[slot, d],
            device_id={"ptl": target, "lib": lax.rem(lib + (n_lib - d if back else d), n_lib)},
        )

    onehot = (
        class_ref[...] == lax.broadcasted_iota(jnp.int32, (CLASSES, class_ref.shape[1]), 0)
    ).astype(jnp.bfloat16)

    final_piece = n_pieces - 1

    def step_near(p):
        kinds = ("m",) if p < n_first else ("m", "x")
        for kind in kinds:
            own_copies[(kind, 0, p)].wait()
            for k in range(n_half):
                settle((kind, k, p))
        scores = dot(images_of(gath.at[p], 0), 0) - norms[0]
        if p >= n_first:
            scores = scores + (dot(images_of(extra.at[p - n_first], 0), 1) - norms[1])
        near_part[p] = scores.reshape(n_half, group, -1)
        for k in range(1, n_half):
            near_copy(p, k).start()

    def step_far(p):
        for k in range(n_half):
            settle(("m", n_half + k, p))
        scores = dot(images_of(gath.at[p], n_half), 0) - norms[0]
        far_part[p] = scores.reshape(n_half, group, -1)
        for k in range(1, n_half):
            far_copy(p, k).start()

    def step_agg(p):
        for k in range(1, n_half):
            far_copy(p, k, True).wait_recv()
            far_part[p, 0] = far_part[p, 0] + far_recv[p, k - 1]
        agg_copy(p).start()

    def step_total(p):
        scores = near_part[p, 0]
        for k in range(1, n_half):
            near_copy(p, k, True).wait_recv()
            scores = scores + near_recv[p, k - 1]
        if p < n_first:
            agg_copy(p).wait_recv()
            scores = scores + agg_recv[p]
        scores = scores.T
        peak = jnp.max(scores, axis=0, keepdims=True)
        weights = jnp.exp(scores - peak)
        mass = jnp.sum(weights, axis=0, keepdims=True)
        wide = slice(p * group, (p + 1) * group)
        brief[0, 0, 0:1, wide] = peak
        brief[0, 0, 1:2, wide] = mass
        post[p, 0] = weights.T.astype(jnp.bfloat16)
        for slot in reversed(range(1, n_ptl)):
            post_copy(p, slot).start()
        if p == final_piece:
            for slot in reversed(range(n_ptl)):
                run_loop(0 if slot else 1, n_lib, lambda d: brief_copy(slot, d).start())
        shares = jnp.dot(onehot, weights.astype(jnp.bfloat16), preferred_element_type=jnp.float32)
        mine = slice(p * ROWS, (p + 1) * ROWS)
        for l in range(n_lib):
            share_out[l, :, mine] = shares[:, l * ROWS : (l + 1) * ROWS]
        if p == final_piece:
            run_loop(1, n_lib, lambda d: share_copy(d).start())

    def total_of(slot):
        top = brief[slot, 0, 0:1]
        for d in range(1, n_lib):
            top = jnp.maximum(top, brief[slot, d, 0:1])
        total = jnp.zeros_like(top)
        for d in range(n_lib):
            total = total + brief[slot, d, 1:2] * jnp.exp(brief[slot, d, 0:1] - top)
        return top + jnp.log(total)

    def pick(values, p):
        low = p * group
        mine = values[:, low : low + ROWS]
        for l in range(1, n_lib):
            at = low + l * ROWS
            mine = jnp.where(lib == l, values[:, at : at + ROWS], mine)
        return mine

    def step_post():
        run_loop(1, n_lib, lambda d: brief_copy(0, d, True).wait_recv())
        evidence = total_of(0)
        factors = [jnp.exp(brief[0, d, 0:1] - evidence) for d in range(n_lib)]
        for p in range(n_pieces):
            mine = slice(p * ROWS, (p + 1) * ROWS)
            small_ref[0:1, mine] = pick(evidence, p)
            for d in range(n_lib):
                factor[d : d + 1, mine] = pick(factors[d], p)
        share = share_out[lib] * factor[0:1]
        for d in range(1, n_lib):
            share_copy(d).wait_recv()
            share = share + share_in[d - 1] * factor[d : d + 1]
        small_ref[8 : 8 + CLASSES] = share

    def step_scale():
        for slot in range(1, n_ptl):
            run_loop(0, n_lib, lambda d: brief_copy(slot, d, True).wait_recv())
        scales = [jnp.exp(brief[slot, 0, 0:1] - total_of(slot)) for slot in range(n_ptl)]
        for p in range(n_pieces):
            wide = slice(p * group, (p + 1) * group)
            for slot in range(1, n_ptl):
                post_copy(p, slot, True).wait_recv()
            for slot in range(0, n_ptl, 2):
                pair = post[p, slot : slot + 2].reshape(2 * group, -1).astype(jnp.float32).T
                row = jnp.concatenate([scales[slot][:, wide], scales[slot + 1][:, wide]], axis=1)
                low = (p * n_ptl + slot) * group
                final[:, low : low + 2 * group] = (pair * row).astype(jnp.bfloat16)

    acts = {
        "relay": relay,
        "take": take,
        "near": step_near,
        "far": step_far,
        "agg": step_agg,
        "total": step_total,
    }
    for name, subject in make_steps(events, n_half, n_first, n_pieces):
        acts[name](subject)

    step_post()
    step_scale()
    for event in events:
        if event[1] >= n_half and event[2] >= n_first:
            settle(event)

    run_loop(1, n_lib, lambda d: share_copy(d).wait_send())
    for slot in range(n_ptl):
        run_loop(0 if slot else 1, n_lib, lambda d: brief_copy(slot, d).wait_send())
    for event in events:
        if event[1]:
            z_copy(event).wait_send()
        run_loop(1, n_x, lambda d: x_copy(event, d).wait_send())
        run_loop(0, n_x, lambda d: core_copy(event, d).wait_send())
    for p in range(n_pieces):
        for k in range(1, n_half):
            near_copy(p, k).wait_send()
            if p < n_first:
                far_copy(p, k).wait_send()
        if p < n_first:
            agg_copy(p).wait_send()
        for slot in range(1, n_ptl):
            post_copy(p, slot).wait_send()


def finish(n_ptl, blocks, images, weights, small, sums, evid, share, total, buffer, own, sem, small_sem):
    part_cols = sums.shape[0]
    span = images.shape[1]
    half = n_ptl * part_cols // 2
    z = lax.axis_index("ptl")
    pair = lax.rem(z, n_ptl // 2)
    offset = pair * part_cols - pair_tile(pair, part_cols, half, span) * LANES
    slack = span - part_cols
    block = span // blocks
    copies = [
        pltpu.make_async_copy(small.at[pl.ds(0, 1)], evid, small_sem.at[0]),
        pltpu.make_async_copy(small.at[pl.ds(8, CLASSES)], share, small_sem.at[1]),
    ]
    for copy in copies:
        copy.start()
    ones = jnp.ones((8, weights.shape[1]), jnp.bfloat16)
    totals = lax.dot_general(
        ones, weights[...], (((1,), (1,)), ((), ())), preferred_element_type=jnp.float32
    )
    count = total.shape[1]
    own_total = totals[0:1, 0:count]
    for y in range(1, n_ptl):
        own_total = jnp.where(z == y, totals[0:1, y * count : (y + 1) * count], own_total)
    own[...] = own_total
    copies.append(pltpu.make_async_copy(own, total, small_sem.at[2]))
    copies[-1].start()
    for b in range(blocks):
        cols = slice(b * block, (b + 1) * block)
        buffer[cols] = jnp.dot(
            weights[...], images[:, cols], preferred_element_type=jnp.float32
        ).T
        low = b * block - slack if b else 0
        size = (b + 1) * block - slack - low
        copies.append(
            pltpu.make_async_copy(
                buffer.at[pl.ds(pl.multiple_of(offset + low, 8), size)],
                sums.at[pl.ds(low, size)],
                sem.at[b],
            )
        )
        copies[-1].start()
    for copy in copies:
        copy.wait()


def trig_table(half):
    index = np.arange(half)
    angle_x = (index % 64) * (2.0 * math.pi / 128.0)
    angle_y = (index // 64) * (2.0 * math.pi / 128.0)
    table = np.zeros((8, half), np.float32)
    table[0], table[1] = np.cos(angle_x), np.sin(angle_x)
    table[2], table[3] = np.cos(angle_y), np.sin(angle_y)
    return table


def on_device(n_lib, n_ptl, particles, shifts, references, inv_noise, proj_class):
    rows, width = particles.shape
    projections = references.shape[0]
    half = width // 2
    part_cols = width // n_ptl
    n_half = n_ptl // 2
    n_x = n_lib // 2
    cover = 0
    for pair in range(n_half):
        cover = max(cover, -(-(pair * part_cols % LANES + part_cols) // LANES))
    span = min(cover * LANES, half)
    n_pieces = rows // ROWS
    n_first = 1
    n_last = n_pieces - n_first
    group = n_lib * ROWS
    own_total = projections // n_ptl
    n_events = len(make_events(n_half, n_first, n_pieces))
    blocks = 5 if (span // LANES) % 5 == 0 else 1
    vmem = pl.BlockSpec(memory_space=pltpu.VMEM)
    far = pl.BlockSpec(memory_space=pltpu.HBM)
    dma = pltpu.SemaphoreType.DMA
    score = (group, projections)
    held_bytes = 2 * n_pieces * n_ptl * group * (span + projections)
    mib = 1024 * 1024
    vmem_limit = (55 - held_bytes // mib) * mib
    images, weights, small = pl.pallas_call(
        functools.partial(kernel, n_lib, n_ptl, span, n_first),
        out_shape=(
            pltpu.VMEM((n_pieces, n_ptl, n_lib, ROWS, span), jnp.bfloat16),
            pltpu.VMEM((projections, n_pieces * n_ptl * group), jnp.bfloat16),
            pltpu.VMEM((8 + CLASSES, rows), jnp.float32),
        ),
        in_specs=[far] * 6,
        out_specs=(vmem, vmem, vmem),
        scratch_shapes=[
            pltpu.VMEM((1, rows), jnp.int32),
            pltpu.VMEM((8, half), jnp.float32),
            pltpu.VMEM((half // LANES, LANES), jnp.float32),
            pltpu.VMEM((1, projections), jnp.int32),
            pltpu.VMEM((n_pieces, ROWS, width), jnp.bfloat16),
            pltpu.VMEM((n_half, 2, n_pieces, ROWS, span), jnp.bfloat16),
            pltpu.VMEM((n_last, n_half, n_lib, ROWS, span), jnp.bfloat16),
            pltpu.VMEM((2, projections, span), jnp.bfloat16),
            pltpu.VMEM((2, projections, span), jnp.bfloat16),
            pltpu.VMEM((1, half), jnp.float32),
            pltpu.VMEM((n_pieces, n_half, *score), jnp.float32),
            pltpu.VMEM((n_pieces, n_half - 1, *score), jnp.float32),
            pltpu.VMEM((n_first, n_half, *score), jnp.float32),
            pltpu.VMEM((n_first, n_half - 1, *score), jnp.float32),
            pltpu.VMEM((n_first, *score), jnp.float32),
            pltpu.VMEM((n_lib, CLASSES, rows), jnp.float32),
            pltpu.VMEM((n_lib - 1, CLASSES, rows), jnp.float32),
            pltpu.VMEM((n_lib, rows), jnp.float32),
            pltpu.VMEM((n_ptl, n_lib, 2, n_pieces * group), jnp.float32),
            pltpu.VMEM((n_pieces, n_ptl, group, projections), jnp.bfloat16),
            dma((4,)),
            dma((n_pieces,)),
            dma((2,)),
            dma((n_events,)),
            dma((n_events,)),
            dma((n_events,)),
            dma((n_events, n_x - 1)),
            dma((n_events, n_x - 1)),
            dma((n_events, n_x)),
            dma((n_events, n_x)),
            dma((n_pieces, n_half - 1)),
            dma((n_pieces, n_half - 1)),
            dma((n_first, n_half - 1)),
            dma((n_first, n_half - 1)),
            dma((n_first,)),
            dma((n_first,)),
            dma((n_lib - 1,)),
            dma((n_lib - 1,)),
            dma((n_pieces, n_ptl - 1)),
            dma((n_pieces, n_ptl - 1)),
            dma((n_ptl, n_lib)),
            dma((n_ptl, n_lib)),
        ],
        compiler_params=pltpu.CompilerParams(
            collective_id=0, has_side_effects=True, vmem_limit_bytes=vmem_limit
        ),
    )(
        particles,
        shifts[None, :],
        trig_table(half),
        references,
        inv_noise.reshape(-1, LANES),
        proj_class[None, :],
    )
    total_rows = n_pieces * n_ptl * group
    sums, evidence, share, total = pl.pallas_call(
        functools.partial(finish, n_ptl, blocks),
        out_shape=(
            pltpu.HBM((part_cols, projections), jnp.float32),
            pltpu.HBM((1, rows), jnp.float32),
            pltpu.HBM((CLASSES, rows), jnp.float32),
            pltpu.HBM((1, own_total), jnp.float32),
        ),
        in_specs=[vmem, vmem, vmem],
        out_specs=(far, far, far, far),
        scratch_shapes=[
            pltpu.VMEM((span, projections), jnp.float32),
            pltpu.VMEM((1, own_total), jnp.float32),
            dma((blocks,)),
            dma((3,)),
        ],
        compiler_params=pltpu.CompilerParams(vmem_limit_bytes=24 * mib),
    )(images.reshape(total_rows, span), weights, small)
    return evidence[0], share.T, sums.T, total[0]


def solution(mesh):
    in_specs = (
        P(("grp", "lib", "ptl"), None),
        P(("grp", "lib", "ptl")),
        P(("grp", "lib"), None),
        P("grp"),
        P("lib"),
    )
    out_specs = (
        P(("grp", "lib", "ptl")),
        P(("grp", "lib", "ptl"), None),
        P(("grp", "lib"), "ptl"),
        P(("grp", "lib", "ptl")),
    )
    return jax.shard_map(
        functools.partial(on_device, mesh.shape["lib"], mesh.shape["ptl"]),
        mesh=mesh,
        in_specs=in_specs,
        out_specs=out_specs,
        check_vma=False,
    )
```

```python
import functools
import math

import jax
import jax.numpy as jnp
import numpy as np
from jax import lax
from jax.experimental import pallas as pl
from jax.experimental.pallas import tpu as pltpu
from jax.sharding import PartitionSpec as P

CLASSES = 16
LANES = 128
ROWS = 16
LAG = 3
AHEAD = (1.0, 1.0)
TOTAL_AT = 2.0
EARLY_AT = 2.2
AGG_AT = 2.0
FIRST_AT = 3.0
CLOSE_AT = 4


def run_loop(low, high, body):
    if high - low <= 4:
        for index in range(low, high):
            body(index)
    else:

        def step(index, carry):
            body(index)
            return carry

        lax.fori_loop(low, high, step, 0)


def diagonal(count):
    shape = (count, count)
    return lax.broadcasted_iota(jnp.int32, shape, 0) == lax.broadcasted_iota(jnp.int32, shape, 1)


def to_column(row):
    return jnp.sum(jnp.where(diagonal(row.shape[1]), row, 0.0), axis=1, keepdims=True)


def to_row(column):
    return jnp.sum(jnp.where(diagonal(column.shape[0]), column, 0.0), axis=0, keepdims=True)


def pair_tile(pair, part_cols, half, span):
    return jnp.minimum((pair * part_cols) // LANES, (half - span) // LANES)


def make_sends(n_half, n_first, n_pieces):
    first, last = range(n_first), range(n_first, n_pieces)
    near = [("m", k, p) for p in first for k in range(1, n_half)]
    near += [(kind, k, p) for p in last for k in range(1, n_half) for kind in ("m", "x")]
    far = [("m", n_half + k, p) for p in first for k in range(n_half)]
    late = [("m", n_half + k, p) for p in last for k in range(n_half)]
    count = len(first) * (n_half - 1)
    return near[:count] + far + near[count:] + late


def make_events(n_half, n_first, n_pieces):
    first, last = range(n_first), range(n_first, n_pieces)
    sends = make_sends(n_half, n_first, n_pieces)
    own = [("m", 0, p) for p in first]
    fill = [(kind, 0, p) for p in last for kind in ("m", "x")]
    early = len(fill) // 2
    return own + fill[:early] + sends[: n_half - 1] + fill[early:] + sends[n_half - 1 :]


def make_steps(events, n_half, n_first, n_pieces):
    number = {event: index for index, event in enumerate(events)}
    count = len(events)
    steps = [(index, "relay", event) for index, event in enumerate(events)]
    for index, event in enumerate(events[LAG:]):
        at = index if index + LAG < count - len(AHEAD) else index - AHEAD[index + LAG - count]
        steps.append((at + 0.1, "take", event))
    totals = []
    for p in range(n_pieces):
        kinds = ("m",) if p < n_first else ("m", "x")
        need = max(number[(kind, k, p)] for kind in kinds for k in range(n_half))
        steps.append((need + 0.5, "near", p))
        total = need + 0.5 + (TOTAL_AT if p == n_pieces - 1 else EARLY_AT)
        if p < n_first:
            need = max(number[("m", n_half + k, p)] for k in range(n_half))
            steps.append((need + 0.6, "far", p))
            steps.append((need + 0.6 + AGG_AT, "agg", p))
            total = max(total, need + 0.6 + AGG_AT + FIRST_AT)
        totals.append(total)
    totals[-1] = max(totals[-1], max(totals) + 0.01)
    steps += [(total, "total", p) for p, total in enumerate(totals)]
    steps.sort(key=lambda step: step[0])
    return [step[1:] for step in steps]


def kernel(
    n_lib,
    n_ptl,
    span,
    n_first,
    part_hbm,
    shift_hbm,
    table_hbm,
    refs_hbm,
    noise_hbm,
    class_hbm,
    gath,
    final,
    small_ref,
    shift_ref,
    table_ref,
    noise_ref,
    class_ref,
    part_ref,
    shifted,
    extra,
    refbuf,
    weighted,
    noise_row,
    near_part,
    near_recv,
    far_part,
    far_recv,
    agg_recv,
    share_out,
    share_in,
    factor,
    lines,
    raw,
    brief,
    post,
    in_sem,
    part_sem,
    ref_sem,
    own_sem,
    z_send,
    z_recv,
    x_send,
    x_recv,
    c_send,
    c_recv,
    n_send,
    n_recv,
    f_send,
    f_recv,
    g_send,
    g_recv,
    t_send,
    t_recv,
    p_send,
    p_recv,
    b_send,
    b_recv,
):
    lib = lax.axis_index("lib")
    ptl = lax.axis_index("ptl")
    n_x = n_lib // 2
    n_half = n_ptl // 2
    x, core = lib // 2, lib % 2
    mate = 2 * x + 1 - core
    local = lax.rem(ptl, n_half)
    side = ptl // n_half
    n_pieces, _, width = part_ref.shape
    half = width // 2
    part_cols = width // n_ptl
    n_last = n_pieces - n_first
    group = n_lib * ROWS
    tiles = span // LANES

    def near_to(k):
        return side * n_half + lax.rem(local + k, n_half)

    def near_from(k):
        return side * n_half + lax.rem(local + n_half - k, n_half)

    def far_to(k):
        return (1 - side) * n_half + lax.rem(local + k, n_half)

    def far_from(k):
        return (1 - side) * n_half + lax.rem(local + n_half - k, n_half)

    in_copies = [
        pltpu.make_async_copy(source, target, in_sem.at[i])
        for i, (source, target) in enumerate(
            (
                (shift_hbm, shift_ref),
                (table_hbm, table_ref),
                (noise_hbm, noise_ref),
                (class_hbm, class_ref),
            )
        )
    ]
    for copy in in_copies:
        copy.start()
    part_copies = [
        pltpu.make_async_copy(part_hbm.at[pl.ds(p * ROWS, ROWS)], part_ref.at[p], part_sem.at[p])
        for p in range(n_pieces)
    ]
    for copy in part_copies:
        copy.start()
    barrier = pltpu.get_barrier_semaphore()

    def greet_ptl(step):
        pl.semaphore_signal(barrier, inc=1, device_id={"ptl": lax.rem(ptl + step, n_ptl)})

    def greet_lib(step):
        pl.semaphore_signal(barrier, inc=1, device_id={"lib": lax.rem(lib + step, n_lib)})

    run_loop(1, n_ptl, greet_ptl)
    run_loop(1, n_lib, greet_lib)

    own_tile = pair_tile(local, part_cols, half, span)

    def chunk_at(tile):
        return pl.ds(pl.multiple_of(tile * LANES, LANES), span)

    side_tiles = (half // LANES) * side
    ref_copies = [
        pltpu.make_async_copy(
            refs_hbm.at[:, chunk_at(own_tile + (side_tiles if b == 0 else half // LANES - side_tiles))],
            refbuf.at[b],
            ref_sem.at[b],
        )
        for b in range(2)
    ]

    in_copies[0].wait()
    in_copies[1].wait()
    ids = to_column(shift_ref[...].astype(jnp.float32)).astype(jnp.int32)
    step_y = (ids >= 3).astype(jnp.int32) + (ids >= 6).astype(jnp.int32)
    step_x = (ids - 3 * step_y - 1).astype(jnp.float32)
    step_y = (step_y - 1).astype(jnp.float32)
    cos_x = jnp.where(step_x == 0.0, 1.0, table_ref[0:1, 0:LANES])
    sin_x = step_x * table_ref[1:2, 0:LANES]

    def shift(k, p):
        first = pair_tile(lax.rem(local + k, n_half), part_cols, half, span)
        rows = slice(p * ROWS, (p + 1) * ROWS)
        zero_y, turn_y = step_y[rows] == 0.0, step_y[rows]
        cx, sx = cos_x[rows], sin_x[rows]
        for tile in range(tiles):
            at = pl.multiple_of((first + tile) * LANES, LANES)
            lo, hi = pl.ds(at, LANES), pl.ds(pl.multiple_of(at + half, LANES), LANES)
            cos_y = jnp.where(zero_y, 1.0, table_ref[2:3, lo])
            sin_y = turn_y * table_ref[3:4, lo]
            cosine = cx * cos_y - sx * sin_y
            sine = sx * cos_y + cx * sin_y
            real = part_ref[p, :, lo].astype(jnp.float32)
            imag = part_ref[p, :, hi].astype(jnp.float32)
            to = slice(tile * LANES, (tile + 1) * LANES)
            shifted[k, 0, p, :, to] = (real * cosine + imag * sine).astype(jnp.bfloat16)
            shifted[k, 1, p, :, to] = (imag * cosine - real * sine).astype(jnp.bfloat16)

    events = make_events(n_half, n_first, n_pieces)
    number = {event: index for index, event in enumerate(events)}

    def place(event, source):
        kind, slot, p = event
        return gath.at[p, slot, source] if kind == "m" else extra.at[p - n_first, slot, source]

    def which(event):
        kind, slot, _ = event
        return side if (kind == "m") == (slot < n_half) else 1 - side

    def z_copy(event, back=False):
        kind, slot, p = event
        k = slot % n_half
        target = (near_from(k) if back else near_to(k)) if slot < n_half else (
            far_from(k) if back else far_to(k)
        )
        return pltpu.make_async_remote_copy(
            src_ref=shifted.at[k, which(event), p],
            dst_ref=place(event, lib),
            send_sem=z_send.at[number[event]],
            recv_sem=z_recv.at[number[event]],
            device_id={"ptl": target},
        )

    def x_source(d):
        return lax.rem(x - d + n_x, n_x) * 2 + core

    def lib_copy(event, d, source, send, recv, to):
        here = source is lib and event[1] == 0
        return pltpu.make_async_remote_copy(
            src_ref=shifted.at[0, which(event), event[2]] if here else place(event, source),
            dst_ref=place(event, source),
            send_sem=send.at[number[event], d],
            recv_sem=recv.at[number[event], d],
            device_id={"lib": to},
        )

    def x_copy(event, d):
        return lib_copy(event, d - 1, lib, x_send, x_recv, lax.rem(x + d, n_x) * 2 + core)

    def x_arrival(event, d):
        return lib_copy(event, d - 1, x_source(d), x_send, x_recv, x_source(d))

    def core_copy(event, d):
        return lib_copy(event, d, lib if isinstance(d, int) and d == 0 else x_source(d), c_send, c_recv, mate)

    def core_arrival(event, d):
        return lib_copy(event, d, x_source(d) + 1 - 2 * core, c_send, c_recv, mate)

    def spread(event):
        run_loop(1, n_x, lambda d: x_copy(event, d).start())
        core_copy(event, 0).start()

    def take(event):
        if event[1]:
            z_copy(event, True).wait_recv()
        spread(event)

    def relay(event):
        def forward(d):
            x_arrival(event, d).wait_recv()
            core_copy(event, d).start()

        run_loop(1, n_x, forward)

    def settle(event):
        run_loop(0, n_x, lambda d: core_arrival(event, d).wait_recv())

    own_copies = {}

    def keep(event):
        own_copies[event] = pltpu.make_async_copy(
            shifted.at[0, which(event), event[2]], place(event, lib), own_sem.at[number[event]]
        )
        own_copies[event].start()

    ready, queue = set(), make_sends(n_half, n_first, n_pieces)
    taken = events[:LAG]

    def issue():
        while queue and (queue[0][1] % n_half, queue[0][2]) in ready:
            z_copy(queue.pop(0)).start()
        while taken and (0, taken[0][2]) in ready:
            take(taken.pop(0))

    for p in range(n_pieces):
        part_copies[p].wait()
        for k in range(n_half):
            shift(k, p)
            if not ready:
                pl.semaphore_wait(barrier, n_ptl - 1 + n_lib - 1)
            ready.add((k, p))
            issue()
            if len(ready) == 1:
                for copy in ref_copies:
                    copy.start()
        keep(("m", 0, p))
        if p >= n_first:
            keep(("x", 0, p))

    in_copies[2].wait()
    in_copies[3].wait()
    for tile in range(half // LANES):
        noise_row[:, tile * LANES : (tile + 1) * LANES] = noise_ref[tile : tile + 1, :]
    offset = local * part_cols - own_tile * LANES
    spot = lax.broadcasted_iota(jnp.int32, (1, span), 1)
    inside = (spot >= offset) & (spot < offset + part_cols)
    noise = jnp.where(inside, noise_row[:, chunk_at(own_tile)], 0.0)
    norms = []
    for b in range(2):
        ref_copies[b].wait()
        widened = refbuf[b].astype(jnp.float32)
        scaled = widened * noise
        weighted[b] = scaled.astype(jnp.bfloat16)
        norms.append(to_row(0.5 * jnp.sum(widened * scaled, axis=1, keepdims=True)))

    def dot(images, b):
        return lax.dot_general(
            images, weighted[b], (((1,), (1,)), ((), ())), preferred_element_type=jnp.float32
        )

    def images_of(ref, low):
        return ref[low : low + n_half].reshape(n_half * group, span)

    def near_copy(p, k, back=False):
        return pltpu.make_async_remote_copy(
            src_ref=near_part.at[p, k],
            dst_ref=near_recv.at[p, k - 1],
            send_sem=n_send.at[p, k - 1],
            recv_sem=n_recv.at[p, k - 1],
            device_id={"ptl": near_to(k) if back else near_from(k)},
        )

    def far_copy(p, k, back=False):
        return pltpu.make_async_remote_copy(
            src_ref=far_part.at[p, k],
            dst_ref=far_recv.at[p, k - 1],
            send_sem=f_send.at[p, k - 1],
            recv_sem=f_recv.at[p, k - 1],
            device_id={"ptl": near_to(k) if back else near_from(k)},
        )

    def agg_copy(p):
        return pltpu.make_async_remote_copy(
            src_ref=far_part.at[p, 0],
            dst_ref=agg_recv.at[p],
            send_sem=g_send.at[p],
            recv_sem=g_recv.at[p],
            device_id={"ptl": far_to(0)},
        )

    def share_copy(d):
        to = lax.rem(lib + d, n_lib)
        return pltpu.make_async_remote_copy(
            src_ref=share_out.at[to],
            dst_ref=share_in.at[d - 1],
            send_sem=t_send.at[d - 1],
            recv_sem=t_recv.at[d - 1],
            device_id={"lib": to},
        )

    def post_copy(p, slot, back=False):
        k = slot % n_half
        if slot < n_half:
            target = near_from(k) if back else near_to(k)
        else:
            target = far_from(k) if back else far_to(k)
        return pltpu.make_async_remote_copy(
            src_ref=post.at[p, 0],
            dst_ref=post.at[p, slot],
            send_sem=p_send.at[p, slot - 1],
            recv_sem=p_recv.at[p, slot - 1],
            device_id={"ptl": target},
        )

    def brief_copy(slot, d, back=False):
        k = slot % n_half
        if slot < n_half:
            target = near_from(k) if back else near_to(k)
        else:
            target = far_from(k) if back else far_to(k)
        return pltpu.make_async_remote_copy(
            src_ref=brief.at[0, 0],
            dst_ref=brief.at[slot, d],
            send_sem=b_send.at[slot, d],
            recv_sem=b_recv.at[slot, d],
            device_id={"ptl": target, "lib": lax.rem(lib + (n_lib - d if back else d), n_lib)},
        )

    onehot = (
        class_ref[...] == lax.broadcasted_iota(jnp.int32, (CLASSES, class_ref.shape[1]), 0)
    ).astype(jnp.bfloat16)

    final_piece = n_pieces - 1

    def step_near(p):
        kinds = ("m",) if p < n_first else ("m", "x")
        for kind in kinds:
            own_copies[(kind, 0, p)].wait()
            for k in range(n_half):
                settle((kind, k, p))
        scores = dot(images_of(gath.at[p], 0), 0) - norms[0]
        if p >= n_first:
            scores = scores + (dot(images_of(extra.at[p - n_first], 0), 1) - norms[1])
        near_part[p] = scores.reshape(n_half, group, -1)
        for k in range(1, n_half):
            near_copy(p, k).start()

    def step_far(p):
        for k in range(n_half):
            settle(("m", n_half + k, p))
        scores = dot(images_of(gath.at[p], n_half), 0) - norms[0]
        far_part[p] = scores.reshape(n_half, group, -1)
        for k in range(1, n_half):
            far_copy(p, k).start()

    def step_agg(p):
        for k in range(1, n_half):
            far_copy(p, k, True).wait_recv()
            far_copy(p, k).wait_send()
            far_part[p, 0] = far_part[p, 0] + far_recv[p, k - 1]
        agg_copy(p).start()

    def step_total(p):
        scores = near_part[p, 0]
        for k in range(1, n_half):
            near_copy(p, k, True).wait_recv()
            near_copy(p, k).wait_send()
            scores = scores + near_recv[p, k - 1]
        if p < n_first:
            agg_copy(p).wait_recv()
            agg_copy(p).wait_send()
            scores = scores + agg_recv[p]
        scores = scores.T
        peak = jnp.max(scores, axis=0, keepdims=True)
        weights = jnp.exp(scores - peak)
        mass = jnp.sum(weights, axis=0, keepdims=True)
        wide = slice(p * group, (p + 1) * group)
        brief[0, 0, 0:1, wide] = peak
        brief[0, 0, 1:2, wide] = mass
        post[p, 0] = weights.T.astype(jnp.bfloat16)
        for slot in reversed(range(1, n_ptl)):
            post_copy(p, slot).start()
        if p == final_piece:
            for slot in reversed(range(n_ptl)):
                run_loop(0 if slot else 1, n_lib, lambda d: brief_copy(slot, d).start())
        shares = jnp.dot(onehot, weights.astype(jnp.bfloat16), preferred_element_type=jnp.float32)
        mine = slice(p * ROWS, (p + 1) * ROWS)
        for l in range(n_lib):
            share_out[l, :, mine] = shares[:, l * ROWS : (l + 1) * ROWS]
        if p == final_piece:
            run_loop(1, n_lib, lambda d: share_copy(d).start())

    def total_of(slot):
        top = brief[slot, 0, 0:1]
        for d in range(1, n_lib):
            top = jnp.maximum(top, brief[slot, d, 0:1])
        total = jnp.zeros_like(top)
        for d in range(n_lib):
            total = total + brief[slot, d, 1:2] * jnp.exp(brief[slot, d, 0:1] - top)
        return top + jnp.log(total)

    def pick(values, p):
        low = p * group
        mine = values[:, low : low + ROWS]
        for l in range(1, n_lib):
            at = low + l * ROWS
            mine = jnp.where(lib == l, values[:, at : at + ROWS], mine)
        return mine

    def step_post():
        run_loop(1, n_lib, lambda d: brief_copy(0, d, True).wait_recv())
        evidence = total_of(0)
        for d in range(n_lib):
            lines[d : d + 1] = jnp.exp(brief[0, d, 0:1] - evidence)
        lines[n_lib : n_lib + 1] = evidence
        for p in range(n_pieces):
            mine = slice(p * ROWS, (p + 1) * ROWS)
            factor[:, mine] = pick(lines[...], p)
        small_ref[0:1] = factor[n_lib : n_lib + 1]
        share = share_out[lib] * factor[0:1]
        for d in range(1, n_lib):
            share_copy(d).wait_recv()
            share = share + share_in[d - 1] * factor[d : d + 1]
        small_ref[8 : 8 + CLASSES] = share

    def places(p, slot):
        low = (p * n_ptl + slot) * group
        return slice(low, low + 2 * group)

    def step_turn(p):
        for slot in range(1, n_ptl):
            post_copy(p, slot, True).wait_recv()
            if p < final_piece:
                post_copy(p, slot).wait_send()
        for slot in range(0, n_ptl, 2):
            pair = post[p, slot : slot + 2].reshape(2 * group, -1)
            raw[:, places(p, slot)] = pair.astype(jnp.float32).T

    def step_scale():
        for slot in range(1, n_ptl):
            run_loop(0, n_lib, lambda d: brief_copy(slot, d, True).wait_recv())
        scales = [jnp.exp(brief[slot, 0, 0:1] - total_of(slot)) for slot in range(n_ptl)]
        for p in range(n_pieces):
            wide = slice(p * group, (p + 1) * group)
            for slot in range(0, n_ptl, 2):
                row = jnp.concatenate([scales[slot][:, wide], scales[slot + 1][:, wide]], axis=1)
                at = places(p, slot)
                final[:, at] = (raw[:, at] * row).astype(jnp.bfloat16)

    acts = {
        "relay": relay,
        "take": take,
        "near": step_near,
        "far": step_far,
        "agg": step_agg,
        "total": step_total,
    }
    def close(event):
        run_loop(1, n_x, lambda d: x_copy(event, d).wait_send())
        run_loop(0, n_x, lambda d: core_copy(event, d).wait_send())

    sends = make_sends(n_half, n_first, n_pieces)
    open_events, open_sends = list(events), list(sends)
    for name, subject in make_steps(events, n_half, n_first, n_pieces):
        acts[name](subject)
        if name == "relay" and number[subject] >= CLOSE_AT:
            close(open_events.pop(0))
            for event in open_sends[:1]:
                z_copy(open_sends.pop(0)).wait_send()

    for p in range(n_pieces - 1):
        step_turn(p)
    step_post()
    step_turn(n_pieces - 1)
    step_scale()
    for event in events:
        if event[1] >= n_half and event[2] >= n_first:
            settle(event)

    run_loop(1, n_lib, lambda d: share_copy(d).wait_send())
    for slot in range(n_ptl):
        run_loop(0 if slot else 1, n_lib, lambda d: brief_copy(slot, d).wait_send())
    for event in open_sends:
        z_copy(event).wait_send()
    for event in open_events:
        close(event)
    for slot in range(1, n_ptl):
        post_copy(final_piece, slot).wait_send()


def finish(n_ptl, blocks, images, weights, small, sums, evid, share, total, buffer, own, sem, small_sem):
    part_cols = sums.shape[0]
    span = images.shape[1]
    half = n_ptl * part_cols // 2
    z = lax.axis_index("ptl")
    pair = lax.rem(z, n_ptl // 2)
    offset = pair * part_cols - pair_tile(pair, part_cols, half, span) * LANES
    slack = span - part_cols
    block = span // blocks
    copies = [
        pltpu.make_async_copy(small.at[pl.ds(0, 1)], evid, small_sem.at[0]),
        pltpu.make_async_copy(small.at[pl.ds(8, CLASSES)], share, small_sem.at[1]),
    ]
    for copy in copies:
        copy.start()
    ones = jnp.ones((8, weights.shape[1]), jnp.bfloat16)
    totals = lax.dot_general(
        ones, weights[...], (((1,), (1,)), ((), ())), preferred_element_type=jnp.float32
    )
    count = total.shape[1]
    own_total = totals[0:1, 0:count]
    for y in range(1, n_ptl):
        own_total = jnp.where(z == y, totals[0:1, y * count : (y + 1) * count], own_total)
    own[...] = own_total
    copies.append(pltpu.make_async_copy(own, total, small_sem.at[2]))
    copies[-1].start()
    for b in range(blocks):
        cols = slice(b * block, (b + 1) * block)
        buffer[cols] = jnp.dot(
            weights[...], images[:, cols], preferred_element_type=jnp.float32
        ).T
        low = b * block - slack if b else 0
        size = (b + 1) * block - slack - low
        copies.append(
            pltpu.make_async_copy(
                buffer.at[pl.ds(pl.multiple_of(offset + low, 8), size)],
                sums.at[pl.ds(low, size)],
                sem.at[b],
            )
        )
        copies[-1].start()
    for copy in copies:
        copy.wait()


def trig_table(half):
    index = np.arange(half)
    angle_x = (index % 64) * (2.0 * math.pi / 128.0)
    angle_y = (index // 64) * (2.0 * math.pi / 128.0)
    table = np.zeros((8, half), np.float32)
    table[0], table[1] = np.cos(angle_x), np.sin(angle_x)
    table[2], table[3] = np.cos(angle_y), np.sin(angle_y)
    return table


def on_device(n_lib, n_ptl, particles, shifts, references, inv_noise, proj_class):
    rows, width = particles.shape
    projections = references.shape[0]
    half = width // 2
    part_cols = width // n_ptl
    n_half = n_ptl // 2
    n_x = n_lib // 2
    cover = 0
    for pair in range(n_half):
        cover = max(cover, -(-(pair * part_cols % LANES + part_cols) // LANES))
    span = min(cover * LANES, half)
    n_pieces = rows // ROWS
    n_first = 1
    n_last = n_pieces - n_first
    group = n_lib * ROWS
    own_total = projections // n_ptl
    n_events = len(make_events(n_half, n_first, n_pieces))
    blocks = 5 if (span // LANES) % 5 == 0 else 1
    vmem = pl.BlockSpec(memory_space=pltpu.VMEM)
    far = pl.BlockSpec(memory_space=pltpu.HBM)
    dma = pltpu.SemaphoreType.DMA
    score = (group, projections)
    held_bytes = 2 * n_pieces * n_ptl * group * (span + projections)
    mib = 1024 * 1024
    vmem_limit = (55 - held_bytes // mib) * mib
    images, weights, small = pl.pallas_call(
        functools.partial(kernel, n_lib, n_ptl, span, n_first),
        out_shape=(
            pltpu.VMEM((n_pieces, n_ptl, n_lib, ROWS, span), jnp.bfloat16),
            pltpu.VMEM((projections, n_pieces * n_ptl * group), jnp.bfloat16),
            pltpu.VMEM((8 + CLASSES, rows), jnp.float32),
        ),
        in_specs=[far] * 6,
        out_specs=(vmem, vmem, vmem),
        scratch_shapes=[
            pltpu.VMEM((1, rows), jnp.int32),
            pltpu.VMEM((8, half), jnp.float32),
            pltpu.VMEM((half // LANES, LANES), jnp.float32),
            pltpu.VMEM((1, projections), jnp.int32),
            pltpu.VMEM((n_pieces, ROWS, width), jnp.bfloat16),
            pltpu.VMEM((n_half, 2, n_pieces, ROWS, span), jnp.bfloat16),
            pltpu.VMEM((n_last, n_half, n_lib, ROWS, span), jnp.bfloat16),
            pltpu.VMEM((2, projections, span), jnp.bfloat16),
            pltpu.VMEM((2, projections, span), jnp.bfloat16),
            pltpu.VMEM((1, half), jnp.float32),
            pltpu.VMEM((n_pieces, n_half, *score), jnp.float32),
            pltpu.VMEM((n_pieces, n_half - 1, *score), jnp.float32),
            pltpu.VMEM((n_first, n_half, *score), jnp.float32),
            pltpu.VMEM((n_first, n_half - 1, *score), jnp.float32),
            pltpu.VMEM((n_first, *score), jnp.float32),
            pltpu.VMEM((n_lib, CLASSES, rows), jnp.float32),
            pltpu.VMEM((n_lib - 1, CLASSES, rows), jnp.float32),
            pltpu.VMEM((n_lib + 1, rows), jnp.float32),
            pltpu.VMEM((n_lib + 1, n_pieces * group), jnp.float32),
            pltpu.VMEM((projections, n_pieces * n_ptl * group), jnp.float32),
            pltpu.VMEM((n_ptl, n_lib, 2, n_pieces * group), jnp.float32),
            pltpu.VMEM((n_pieces, n_ptl, group, projections), jnp.bfloat16),
            dma((4,)),
            dma((n_pieces,)),
            dma((2,)),
            dma((n_events,)),
            dma((n_events,)),
            dma((n_events,)),
            dma((n_events, n_x - 1)),
            dma((n_events, n_x - 1)),
            dma((n_events, n_x)),
            dma((n_events, n_x)),
            dma((n_pieces, n_half - 1)),
            dma((n_pieces, n_half - 1)),
            dma((n_first, n_half - 1)),
            dma((n_first, n_half - 1)),
            dma((n_first,)),
            dma((n_first,)),
            dma((n_lib - 1,)),
            dma((n_lib - 1,)),
            dma((n_pieces, n_ptl - 1)),
            dma((n_pieces, n_ptl - 1)),
            dma((n_ptl, n_lib)),
            dma((n_ptl, n_lib)),
        ],
        compiler_params=pltpu.CompilerParams(
            collective_id=0, has_side_effects=True, vmem_limit_bytes=vmem_limit
        ),
    )(
        particles,
        shifts[None, :],
        trig_table(half),
        references,
        inv_noise.reshape(-1, LANES),
        proj_class[None, :],
    )
    total_rows = n_pieces * n_ptl * group
    sums, evidence, share, total = pl.pallas_call(
        functools.partial(finish, n_ptl, blocks),
        out_shape=(
            pltpu.HBM((part_cols, projections), jnp.float32),
            pltpu.HBM((1, rows), jnp.float32),
            pltpu.HBM((CLASSES, rows), jnp.float32),
            pltpu.HBM((1, own_total), jnp.float32),
        ),
        in_specs=[vmem, vmem, vmem],
        out_specs=(far, far, far, far),
        scratch_shapes=[
            pltpu.VMEM((span, projections), jnp.float32),
            pltpu.VMEM((1, own_total), jnp.float32),
            dma((blocks,)),
            dma((3,)),
        ],
        compiler_params=pltpu.CompilerParams(vmem_limit_bytes=24 * mib),
    )(images.reshape(total_rows, span), weights, small)
    return evidence[0], share.T, sums.T, total[0]


def solution(mesh):
    in_specs = (
        P(("grp", "lib", "ptl"), None),
        P(("grp", "lib", "ptl")),
        P(("grp", "lib"), None),
        P("grp"),
        P("lib"),
    )
    out_specs = (
        P(("grp", "lib", "ptl")),
        P(("grp", "lib", "ptl"), None),
        P(("grp", "lib"), "ptl"),
        P(("grp", "lib", "ptl")),
    )
    return jax.shard_map(
        functools.partial(on_device, mesh.shape["lib"], mesh.shape["ptl"]),
        mesh=mesh,
        in_specs=in_specs,
        out_specs=out_specs,
        check_vma=False,
    )
```

```python
import functools
import math

import jax
import jax.numpy as jnp
import numpy as np
from jax import lax
from jax.experimental import pallas as pl
from jax.experimental.pallas import tpu as pltpu
from jax.sharding import PartitionSpec as P

CLASSES = 16
LANES = 128
ROWS = 16
LAG = 3
AHEAD = (1.0, 1.0)
TOTAL_AT = 2.0
EARLY_AT = 2.2
AGG_AT = 2.0
FIRST_AT = 2.5
CLOSE_AT = 4


def run_loop(low, high, body):
    if high - low <= 4:
        for index in range(low, high):
            body(index)
    else:

        def step(index, carry):
            body(index)
            return carry

        lax.fori_loop(low, high, step, 0)


def diagonal(count):
    shape = (count, count)
    return lax.broadcasted_iota(jnp.int32, shape, 0) == lax.broadcasted_iota(jnp.int32, shape, 1)


def to_column(row):
    return jnp.sum(jnp.where(diagonal(row.shape[1]), row, 0.0), axis=1, keepdims=True)


def to_row(column):
    return jnp.sum(jnp.where(diagonal(column.shape[0]), column, 0.0), axis=0, keepdims=True)


def pair_tile(pair, part_cols, half, span):
    return jnp.minimum((pair * part_cols) // LANES, (half - span) // LANES)


def make_sends(n_half, n_first, n_pieces):
    first, last = range(n_first), range(n_first, n_pieces)
    near = [("m", k, p) for p in first for k in range(1, n_half)]
    near += [(kind, k, p) for p in last for k in range(1, n_half) for kind in ("m", "x")]
    far = [("m", n_half + k, p) for p in first for k in range(n_half)]
    late = [("m", n_half + k, p) for p in last for k in range(n_half)]
    count = len(first) * (n_half - 1)
    return near[:count] + far[:n_half + 1] + near[count:] + far[n_half + 1 :] + late


def make_events(n_half, n_first, n_pieces):
    first, last = range(n_first), range(n_first, n_pieces)
    sends = make_sends(n_half, n_first, n_pieces)
    own = [("m", 0, p) for p in first]
    fill = [(kind, 0, p) for p in last for kind in ("m", "x")]
    early = len(fill) // 2
    return own + fill[:early] + sends[: n_half - 1] + fill[early:] + sends[n_half - 1 :]


def make_steps(events, n_half, n_first, n_pieces):
    number = {event: index for index, event in enumerate(events)}
    count = len(events)
    steps = [(index, "relay", event) for index, event in enumerate(events)]
    for index, event in enumerate(events[LAG:]):
        at = index if index + LAG < count - len(AHEAD) else index - AHEAD[index + LAG - count]
        steps.append((at + 0.1, "take", event))
    totals = []
    for p in range(n_pieces):
        kinds = ("m",) if p < n_first else ("m", "x")
        need = max(number[(kind, k, p)] for kind in kinds for k in range(n_half))
        steps.append((need + 0.5, "near", p))
        total = need + 0.5 + (TOTAL_AT if p == n_pieces - 1 else EARLY_AT)
        if p < n_first:
            need = max(number[("m", n_half + k, p)] for k in range(n_half))
            steps.append((need + 0.6, "far", p))
            steps.append((need + 0.6 + AGG_AT, "agg", p))
            total = max(total, need + 0.6 + AGG_AT + FIRST_AT)
        totals.append(total)
    steps += [(total, "total", p) for p, total in enumerate(totals)]
    steps.sort(key=lambda step: step[0])
    return [step[1:] for step in steps]


def kernel(
    n_lib,
    n_ptl,
    span,
    n_first,
    part_hbm,
    shift_hbm,
    table_hbm,
    refs_hbm,
    noise_hbm,
    class_hbm,
    gath,
    final,
    small_ref,
    shift_ref,
    table_ref,
    noise_ref,
    class_ref,
    part_ref,
    shifted,
    extra,
    refbuf,
    weighted,
    noise_row,
    near_part,
    near_recv,
    far_part,
    far_recv,
    agg_recv,
    share_out,
    share_in,
    factor,
    lines,
    raw,
    brief,
    post,
    in_sem,
    part_sem,
    ref_sem,
    own_sem,
    z_send,
    z_recv,
    x_send,
    x_recv,
    c_send,
    c_recv,
    n_send,
    n_recv,
    f_send,
    f_recv,
    g_send,
    g_recv,
    t_send,
    t_recv,
    p_send,
    p_recv,
    b_send,
    b_recv,
):
    lib = lax.axis_index("lib")
    ptl = lax.axis_index("ptl")
    n_x = n_lib // 2
    n_half = n_ptl // 2
    x, core = lib // 2, lib % 2
    mate = 2 * x + 1 - core
    local = lax.rem(ptl, n_half)
    side = ptl // n_half
    n_pieces, _, width = part_ref.shape
    half = width // 2
    part_cols = width // n_ptl
    n_last = n_pieces - n_first
    group = n_lib * ROWS
    tiles = span // LANES

    def near_to(k):
        return side * n_half + lax.rem(local + k, n_half)

    def near_from(k):
        return side * n_half + lax.rem(local + n_half - k, n_half)

    def far_to(k):
        return (1 - side) * n_half + lax.rem(local + k, n_half)

    def far_from(k):
        return (1 - side) * n_half + lax.rem(local + n_half - k, n_half)

    in_copies = [
        pltpu.make_async_copy(source, target, in_sem.at[i])
        for i, (source, target) in enumerate(
            (
                (shift_hbm, shift_ref),
                (table_hbm, table_ref),
                (noise_hbm, noise_ref),
                (class_hbm, class_ref),
            )
        )
    ]
    for copy in in_copies:
        copy.start()
    part_copies = [
        pltpu.make_async_copy(part_hbm.at[pl.ds(p * ROWS, ROWS)], part_ref.at[p], part_sem.at[p])
        for p in range(n_pieces)
    ]
    for copy in part_copies:
        copy.start()
    barrier = pltpu.get_barrier_semaphore()

    def greet_ptl(step):
        pl.semaphore_signal(barrier, inc=1, device_id={"ptl": lax.rem(ptl + step, n_ptl)})

    def greet_lib(step):
        pl.semaphore_signal(barrier, inc=1, device_id={"lib": lax.rem(lib + step, n_lib)})

    run_loop(1, n_ptl, greet_ptl)
    run_loop(1, n_lib, greet_lib)

    own_tile = pair_tile(local, part_cols, half, span)

    def chunk_at(tile):
        return pl.ds(pl.multiple_of(tile * LANES, LANES), span)

    side_tiles = (half // LANES) * side
    ref_copies = [
        pltpu.make_async_copy(
            refs_hbm.at[:, chunk_at(own_tile + (side_tiles if b == 0 else half // LANES - side_tiles))],
            refbuf.at[b],
            ref_sem.at[b],
        )
        for b in range(2)
    ]

    in_copies[0].wait()
    in_copies[1].wait()
    ids = to_column(shift_ref[...].astype(jnp.float32)).astype(jnp.int32)
    step_y = (ids >= 3).astype(jnp.int32) + (ids >= 6).astype(jnp.int32)
    step_x = (ids - 3 * step_y - 1).astype(jnp.float32)
    step_y = (step_y - 1).astype(jnp.float32)
    cos_x = jnp.where(step_x == 0.0, 1.0, table_ref[0:1, 0:LANES])
    sin_x = step_x * table_ref[1:2, 0:LANES]

    def shift(k, p):
        first = pair_tile(lax.rem(local + k, n_half), part_cols, half, span)
        rows = slice(p * ROWS, (p + 1) * ROWS)
        zero_y, turn_y = step_y[rows] == 0.0, step_y[rows]
        cx, sx = cos_x[rows], sin_x[rows]
        for tile in range(tiles):
            at = pl.multiple_of((first + tile) * LANES, LANES)
            lo, hi = pl.ds(at, LANES), pl.ds(pl.multiple_of(at + half, LANES), LANES)
            cos_y = jnp.where(zero_y, 1.0, table_ref[2:3, lo])
            sin_y = turn_y * table_ref[3:4, lo]
            cosine = cx * cos_y - sx * sin_y
            sine = sx * cos_y + cx * sin_y
            real = part_ref[p, :, lo].astype(jnp.float32)
            imag = part_ref[p, :, hi].astype(jnp.float32)
            to = slice(tile * LANES, (tile + 1) * LANES)
            shifted[k, 0, p, :, to] = (real * cosine + imag * sine).astype(jnp.bfloat16)
            shifted[k, 1, p, :, to] = (imag * cosine - real * sine).astype(jnp.bfloat16)

    events = make_events(n_half, n_first, n_pieces)
    number = {event: index for index, event in enumerate(events)}

    def place(event, source):
        kind, slot, p = event
        return gath.at[p, slot, source] if kind == "m" else extra.at[p - n_first, slot, source]

    def which(event):
        kind, slot, _ = event
        return side if (kind == "m") == (slot < n_half) else 1 - side

    def z_copy(event, back=False):
        kind, slot, p = event
        k = slot % n_half
        target = (near_from(k) if back else near_to(k)) if slot < n_half else (
            far_from(k) if back else far_to(k)
        )
        return pltpu.make_async_remote_copy(
            src_ref=shifted.at[k, which(event), p],
            dst_ref=place(event, lib),
            send_sem=z_send.at[number[event]],
            recv_sem=z_recv.at[number[event]],
            device_id={"ptl": target},
        )

    def x_source(d):
        return lax.rem(x - d + n_x, n_x) * 2 + core

    def lib_copy(event, d, source, send, recv, to):
        here = source is lib and event[1] == 0
        return pltpu.make_async_remote_copy(
            src_ref=shifted.at[0, which(event), event[2]] if here else place(event, source),
            dst_ref=place(event, source),
            send_sem=send.at[number[event], d],
            recv_sem=recv.at[number[event], d],
            device_id={"lib": to},
        )

    def x_copy(event, d):
        return lib_copy(event, d - 1, lib, x_send, x_recv, lax.rem(x + d, n_x) * 2 + core)

    def x_arrival(event, d):
        return lib_copy(event, d - 1, x_source(d), x_send, x_recv, x_source(d))

    def core_copy(event, d):
        return lib_copy(event, d, lib if isinstance(d, int) and d == 0 else x_source(d), c_send, c_recv, mate)

    def core_arrival(event, d):
        return lib_copy(event, d, x_source(d) + 1 - 2 * core, c_send, c_recv, mate)

    def spread(event):
        run_loop(1, n_x, lambda d: x_copy(event, d).start())
        core_copy(event, 0).start()

    def take(event):
        if event[1]:
            z_copy(event, True).wait_recv()
        spread(event)

    def relay(event):
        def forward(d):
            x_arrival(event, d).wait_recv()
            core_copy(event, d).start()

        run_loop(1, n_x, forward)

    def settle(event):
        run_loop(0, n_x, lambda d: core_arrival(event, d).wait_recv())

    own_copies = {}

    def keep(event):
        own_copies[event] = pltpu.make_async_copy(
            shifted.at[0, which(event), event[2]], place(event, lib), own_sem.at[number[event]]
        )
        own_copies[event].start()

    ready, queue = set(), make_sends(n_half, n_first, n_pieces)
    taken = events[:LAG]

    def issue():
        while queue and (queue[0][1] % n_half, queue[0][2]) in ready:
            z_copy(queue.pop(0)).start()
        while taken and (0, taken[0][2]) in ready:
            take(taken.pop(0))

    for p in range(n_pieces):
        part_copies[p].wait()
        for k in range(n_half):
            shift(k, p)
            if not ready:
                pl.semaphore_wait(barrier, n_ptl - 1 + n_lib - 1)
            ready.add((k, p))
            issue()
            if len(ready) == 1:
                for copy in ref_copies:
                    copy.start()
        keep(("m", 0, p))
        if p >= n_first:
            keep(("x", 0, p))

    in_copies[2].wait()
    in_copies[3].wait()
    for tile in range(half // LANES):
        noise_row[:, tile * LANES : (tile + 1) * LANES] = noise_ref[tile : tile + 1, :]
    offset = local * part_cols - own_tile * LANES
    spot = lax.broadcasted_iota(jnp.int32, (1, span), 1)
    inside = (spot >= offset) & (spot < offset + part_cols)
    noise = jnp.where(inside, noise_row[:, chunk_at(own_tile)], 0.0)
    norms = []
    for b in range(2):
        ref_copies[b].wait()
        widened = refbuf[b].astype(jnp.float32)
        scaled = widened * noise
        weighted[b] = scaled.astype(jnp.bfloat16)
        norms.append(to_row(0.5 * jnp.sum(widened * scaled, axis=1, keepdims=True)))

    def dot(images, b):
        return lax.dot_general(
            images, weighted[b], (((1,), (1,)), ((), ())), preferred_element_type=jnp.float32
        )

    def images_of(ref, low):
        return ref[low : low + n_half].reshape(n_half * group, span)

    def near_copy(p, k, back=False):
        return pltpu.make_async_remote_copy(
            src_ref=near_part.at[p, k],
            dst_ref=near_recv.at[p, k - 1],
            send_sem=n_send.at[p, k - 1],
            recv_sem=n_recv.at[p, k - 1],
            device_id={"ptl": near_to(k) if back else near_from(k)},
        )

    def far_copy(p, k, back=False):
        return pltpu.make_async_remote_copy(
            src_ref=far_part.at[p, k],
            dst_ref=far_recv.at[p, k - 1],
            send_sem=f_send.at[p, k - 1],
            recv_sem=f_recv.at[p, k - 1],
            device_id={"ptl": near_to(k) if back else near_from(k)},
        )

    def agg_copy(p):
        return pltpu.make_async_remote_copy(
            src_ref=far_part.at[p, 0],
            dst_ref=agg_recv.at[p],
            send_sem=g_send.at[p],
            recv_sem=g_recv.at[p],
            device_id={"ptl": far_to(0)},
        )

    def share_copy(d):
        to = lax.rem(lib + d, n_lib)
        return pltpu.make_async_remote_copy(
            src_ref=share_out.at[to],
            dst_ref=share_in.at[d - 1],
            send_sem=t_send.at[d - 1],
            recv_sem=t_recv.at[d - 1],
            device_id={"lib": to},
        )

    def post_copy(p, slot, back=False):
        k = slot % n_half
        if slot < n_half:
            target = near_from(k) if back else near_to(k)
        else:
            target = far_from(k) if back else far_to(k)
        return pltpu.make_async_remote_copy(
            src_ref=post.at[p, 0],
            dst_ref=post.at[p, slot],
            send_sem=p_send.at[p, slot - 1],
            recv_sem=p_recv.at[p, slot - 1],
            device_id={"ptl": target},
        )

    def brief_copy(slot, d, back=False):
        k = slot % n_half
        if slot < n_half:
            target = near_from(k) if back else near_to(k)
        else:
            target = far_from(k) if back else far_to(k)
        return pltpu.make_async_remote_copy(
            src_ref=brief.at[0, 0],
            dst_ref=brief.at[slot, d],
            send_sem=b_send.at[slot, d],
            recv_sem=b_recv.at[slot, d],
            device_id={"ptl": target, "lib": lax.rem(lib + (n_lib - d if back else d), n_lib)},
        )

    onehot = (
        class_ref[...] == lax.broadcasted_iota(jnp.int32, (CLASSES, class_ref.shape[1]), 0)
    ).astype(jnp.bfloat16)

    steps = make_steps(events, n_half, n_first, n_pieces)
    final_piece = [subject for name, subject in steps if name == "total"][-1]

    def step_near(p):
        kinds = ("m",) if p < n_first else ("m", "x")
        for kind in kinds:
            own_copies[(kind, 0, p)].wait()
            for k in range(n_half):
                settle((kind, k, p))
        scores = dot(images_of(gath.at[p], 0), 0) - norms[0]
        if p >= n_first:
            scores = scores + (dot(images_of(extra.at[p - n_first], 0), 1) - norms[1])
        near_part[p] = scores.reshape(n_half, group, -1)
        for k in range(1, n_half):
            near_copy(p, k).start()

    def step_far(p):
        for k in range(n_half):
            settle(("m", n_half + k, p))
        scores = dot(images_of(gath.at[p], n_half), 0) - norms[0]
        far_part[p] = scores.reshape(n_half, group, -1)
        for k in range(1, n_half):
            far_copy(p, k).start()

    def step_agg(p):
        for k in range(1, n_half):
            far_copy(p, k, True).wait_recv()
            far_copy(p, k).wait_send()
            far_part[p, 0] = far_part[p, 0] + far_recv[p, k - 1]
        agg_copy(p).start()

    def step_total(p):
        scores = near_part[p, 0]
        for k in range(1, n_half):
            near_copy(p, k, True).wait_recv()
            near_copy(p, k).wait_send()
            scores = scores + near_recv[p, k - 1]
        if p < n_first:
            agg_copy(p).wait_recv()
            agg_copy(p).wait_send()
            scores = scores + agg_recv[p]
        scores = scores.T
        peak = jnp.max(scores, axis=0, keepdims=True)
        weights = jnp.exp(scores - peak)
        mass = jnp.sum(weights, axis=0, keepdims=True)
        wide = slice(p * group, (p + 1) * group)
        brief[0, 0, 0:1, wide] = peak
        brief[0, 0, 1:2, wide] = mass
        post[p, 0] = weights.T.astype(jnp.bfloat16)
        for slot in reversed(range(1, n_ptl)):
            post_copy(p, slot).start()
        if p == final_piece:
            for slot in reversed(range(n_ptl)):
                run_loop(0 if slot else 1, n_lib, lambda d: brief_copy(slot, d).start())
        shares = jnp.dot(onehot, weights.astype(jnp.bfloat16), preferred_element_type=jnp.float32)
        mine = slice(p * ROWS, (p + 1) * ROWS)
        for l in range(n_lib):
            share_out[l, :, mine] = shares[:, l * ROWS : (l + 1) * ROWS]
        if p == final_piece:
            run_loop(1, n_lib, lambda d: share_copy(d).start())

    def total_of(slot):
        top = brief[slot, 0, 0:1]
        for d in range(1, n_lib):
            top = jnp.maximum(top, brief[slot, d, 0:1])
        total = jnp.zeros_like(top)
        for d in range(n_lib):
            total = total + brief[slot, d, 1:2] * jnp.exp(brief[slot, d, 0:1] - top)
        return top + jnp.log(total)

    def pick(values, p):
        low = p * group
        mine = values[:, low : low + ROWS]
        for l in range(1, n_lib):
            at = low + l * ROWS
            mine = jnp.where(lib == l, values[:, at : at + ROWS], mine)
        return mine

    def step_post():
        run_loop(1, n_lib, lambda d: brief_copy(0, d, True).wait_recv())
        evidence = total_of(0)
        for d in range(n_lib):
            lines[d : d + 1] = jnp.exp(brief[0, d, 0:1] - evidence)
        lines[n_lib : n_lib + 1] = evidence
        for p in range(n_pieces):
            mine = slice(p * ROWS, (p + 1) * ROWS)
            factor[:, mine] = pick(lines[...], p)
        small_ref[0:1] = factor[n_lib : n_lib + 1]
        share = share_out[lib] * factor[0:1]
        for d in range(1, n_lib):
            share_copy(d).wait_recv()
            share = share + share_in[d - 1] * factor[d : d + 1]
        small_ref[8 : 8 + CLASSES] = share

    def places(p, slot):
        low = (p * n_ptl + slot) * group
        return slice(low, low + 2 * group)

    def step_turn(p):
        for slot in range(1, n_ptl):
            post_copy(p, slot, True).wait_recv()
            if p != final_piece:
                post_copy(p, slot).wait_send()
        for slot in range(0, n_ptl, 2):
            pair = post[p, slot : slot + 2].reshape(2 * group, -1)
            raw[:, places(p, slot)] = pair.astype(jnp.float32).T

    def step_scale():
        for slot in range(1, n_ptl):
            run_loop(0, n_lib, lambda d: brief_copy(slot, d, True).wait_recv())
        scales = [jnp.exp(brief[slot, 0, 0:1] - total_of(slot)) for slot in range(n_ptl)]
        for p in range(n_pieces):
            wide = slice(p * group, (p + 1) * group)
            for slot in range(0, n_ptl, 2):
                row = jnp.concatenate([scales[slot][:, wide], scales[slot + 1][:, wide]], axis=1)
                at = places(p, slot)
                final[:, at] = (raw[:, at] * row).astype(jnp.bfloat16)

    acts = {
        "relay": relay,
        "take": take,
        "near": step_near,
        "far": step_far,
        "agg": step_agg,
        "total": step_total,
    }
    def close(event):
        run_loop(1, n_x, lambda d: x_copy(event, d).wait_send())
        run_loop(0, n_x, lambda d: core_copy(event, d).wait_send())

    sends = make_sends(n_half, n_first, n_pieces)
    open_events, open_sends = list(events), list(sends)
    for name, subject in steps:
        acts[name](subject)
        if name == "relay" and number[subject] >= CLOSE_AT:
            close(open_events.pop(0))
            for event in open_sends[:1]:
                z_copy(open_sends.pop(0)).wait_send()

    for p in range(n_pieces):
        if p != final_piece:
            step_turn(p)
    step_post()
    step_turn(final_piece)
    step_scale()
    for event in events:
        if event[1] >= n_half and event[2] >= n_first:
            settle(event)

    run_loop(1, n_lib, lambda d: share_copy(d).wait_send())
    for slot in range(n_ptl):
        run_loop(0 if slot else 1, n_lib, lambda d: brief_copy(slot, d).wait_send())
    for event in open_sends:
        z_copy(event).wait_send()
    for event in open_events:
        close(event)
    for slot in range(1, n_ptl):
        post_copy(final_piece, slot).wait_send()


def finish(n_ptl, blocks, images, weights, small, sums, evid, share, total, buffer, own, sem, small_sem):
    part_cols = sums.shape[0]
    span = images.shape[1]
    half = n_ptl * part_cols // 2
    z = lax.axis_index("ptl")
    pair = lax.rem(z, n_ptl // 2)
    offset = pair * part_cols - pair_tile(pair, part_cols, half, span) * LANES
    slack = span - part_cols
    block = span // blocks
    copies = [
        pltpu.make_async_copy(small.at[pl.ds(0, 1)], evid, small_sem.at[0]),
        pltpu.make_async_copy(small.at[pl.ds(8, CLASSES)], share, small_sem.at[1]),
    ]
    for copy in copies:
        copy.start()
    ones = jnp.ones((8, weights.shape[1]), jnp.bfloat16)
    totals = lax.dot_general(
        ones, weights[...], (((1,), (1,)), ((), ())), preferred_element_type=jnp.float32
    )
    count = total.shape[1]
    own_total = totals[0:1, 0:count]
    for y in range(1, n_ptl):
        own_total = jnp.where(z == y, totals[0:1, y * count : (y + 1) * count], own_total)
    own[...] = own_total
    copies.append(pltpu.make_async_copy(own, total, small_sem.at[2]))
    copies[-1].start()
    for b in range(blocks):
        cols = slice(b * block, (b + 1) * block)
        buffer[cols] = jnp.dot(
            weights[...], images[:, cols], preferred_element_type=jnp.float32
        ).T
        low = b * block - slack if b else 0
        size = (b + 1) * block - slack - low
        copies.append(
            pltpu.make_async_copy(
                buffer.at[pl.ds(pl.multiple_of(offset + low, 8), size)],
                sums.at[pl.ds(low, size)],
                sem.at[b],
            )
        )
        copies[-1].start()
    for copy in copies:
        copy.wait()


def trig_table(half):
    index = np.arange(half)
    angle_x = (index % 64) * (2.0 * math.pi / 128.0)
    angle_y = (index // 64) * (2.0 * math.pi / 128.0)
    table = np.zeros((8, half), np.float32)
    table[0], table[1] = np.cos(angle_x), np.sin(angle_x)
    table[2], table[3] = np.cos(angle_y), np.sin(angle_y)
    return table


def on_device(n_lib, n_ptl, particles, shifts, references, inv_noise, proj_class):
    rows, width = particles.shape
    projections = references.shape[0]
    half = width // 2
    part_cols = width // n_ptl
    n_half = n_ptl // 2
    n_x = n_lib // 2
    cover = 0
    for pair in range(n_half):
        cover = max(cover, -(-(pair * part_cols % LANES + part_cols) // LANES))
    span = min(cover * LANES, half)
    n_pieces = rows // ROWS
    n_first = 1
    n_last = n_pieces - n_first
    group = n_lib * ROWS
    own_total = projections // n_ptl
    n_events = len(make_events(n_half, n_first, n_pieces))
    blocks = 5 if (span // LANES) % 5 == 0 else 1
    vmem = pl.BlockSpec(memory_space=pltpu.VMEM)
    far = pl.BlockSpec(memory_space=pltpu.HBM)
    dma = pltpu.SemaphoreType.DMA
    score = (group, projections)
    held_bytes = 2 * n_pieces * n_ptl * group * (span + projections)
    mib = 1024 * 1024
    vmem_limit = (55 - held_bytes // mib) * mib
    images, weights, small = pl.pallas_call(
        functools.partial(kernel, n_lib, n_ptl, span, n_first),
        out_shape=(
            pltpu.VMEM((n_pieces, n_ptl, n_lib, ROWS, span), jnp.bfloat16),
            pltpu.VMEM((projections, n_pieces * n_ptl * group), jnp.bfloat16),
            pltpu.VMEM((8 + CLASSES, rows), jnp.float32),
        ),
        in_specs=[far] * 6,
        out_specs=(vmem, vmem, vmem),
        scratch_shapes=[
            pltpu.VMEM((1, rows), jnp.int32),
            pltpu.VMEM((8, half), jnp.float32),
            pltpu.VMEM((half // LANES, LANES), jnp.float32),
            pltpu.VMEM((1, projections), jnp.int32),
            pltpu.VMEM((n_pieces, ROWS, width), jnp.bfloat16),
            pltpu.VMEM((n_half, 2, n_pieces, ROWS, span), jnp.bfloat16),
            pltpu.VMEM((n_last, n_half, n_lib, ROWS, span), jnp.bfloat16),
            pltpu.VMEM((2, projections, span), jnp.bfloat16),
            pltpu.VMEM((2, projections, span), jnp.bfloat16),
            pltpu.VMEM((1, half), jnp.float32),
            pltpu.VMEM((n_pieces, n_half, *score), jnp.float32),
            pltpu.VMEM((n_pieces, n_half - 1, *score), jnp.float32),
            pltpu.VMEM((n_first, n_half, *score), jnp.float32),
            pltpu.VMEM((n_first, n_half - 1, *score), jnp.float32),
            pltpu.VMEM((n_first, *score), jnp.float32),
            pltpu.VMEM((n_lib, CLASSES, rows), jnp.float32),
            pltpu.VMEM((n_lib - 1, CLASSES, rows), jnp.float32),
            pltpu.VMEM((n_lib + 1, rows), jnp.float32),
            pltpu.VMEM((n_lib + 1, n_pieces * group), jnp.float32),
            pltpu.VMEM((projections, n_pieces * n_ptl * group), jnp.float32),
            pltpu.VMEM((n_ptl, n_lib, 2, n_pieces * group), jnp.float32),
            pltpu.VMEM((n_pieces, n_ptl, group, projections), jnp.bfloat16),
            dma((4,)),
            dma((n_pieces,)),
            dma((2,)),
            dma((n_events,)),
            dma((n_events,)),
            dma((n_events,)),
            dma((n_events, n_x - 1)),
            dma((n_events, n_x - 1)),
            dma((n_events, n_x)),
            dma((n_events, n_x)),
            dma((n_pieces, n_half - 1)),
            dma((n_pieces, n_half - 1)),
            dma((n_first, n_half - 1)),
            dma((n_first, n_half - 1)),
            dma((n_first,)),
            dma((n_first,)),
            dma((n_lib - 1,)),
            dma((n_lib - 1,)),
            dma((n_pieces, n_ptl - 1)),
            dma((n_pieces, n_ptl - 1)),
            dma((n_ptl, n_lib)),
            dma((n_ptl, n_lib)),
        ],
        compiler_params=pltpu.CompilerParams(
            collective_id=0, has_side_effects=True, vmem_limit_bytes=vmem_limit
        ),
    )(
        particles,
        shifts[None, :],
        trig_table(half),
        references,
        inv_noise.reshape(-1, LANES),
        proj_class[None, :],
    )
    total_rows = n_pieces * n_ptl * group
    sums, evidence, share, total = pl.pallas_call(
        functools.partial(finish, n_ptl, blocks),
        out_shape=(
            pltpu.HBM((part_cols, projections), jnp.float32),
            pltpu.HBM((1, rows), jnp.float32),
            pltpu.HBM((CLASSES, rows), jnp.float32),
            pltpu.HBM((1, own_total), jnp.float32),
        ),
        in_specs=[vmem, vmem, vmem],
        out_specs=(far, far, far, far),
        scratch_shapes=[
            pltpu.VMEM((span, projections), jnp.float32),
            pltpu.VMEM((1, own_total), jnp.float32),
            dma((blocks,)),
            dma((3,)),
        ],
        compiler_params=pltpu.CompilerParams(vmem_limit_bytes=24 * mib),
    )(images.reshape(total_rows, span), weights, small)
    return evidence[0], share.T, sums.T, total[0]


def solution(mesh):
    in_specs = (
        P(("grp", "lib", "ptl"), None),
        P(("grp", "lib", "ptl")),
        P(("grp", "lib"), None),
        P("grp"),
        P("lib"),
    )
    out_specs = (
        P(("grp", "lib", "ptl")),
        P(("grp", "lib", "ptl"), None),
        P(("grp", "lib"), "ptl"),
        P(("grp", "lib", "ptl")),
    )
    return jax.shard_map(
        functools.partial(on_device, mesh.shape["lib"], mesh.shape["ptl"]),
        mesh=mesh,
        in_specs=in_specs,
        out_specs=out_specs,
        check_vma=False,
    )
```

```python
import functools
import math

import jax
import jax.numpy as jnp
import numpy as np
from jax import lax
from jax.experimental import pallas as pl
from jax.experimental.pallas import tpu as pltpu
from jax.sharding import PartitionSpec as P

CLASSES = 16
LANES = 128
ROWS = 16
LAG = 3
AHEAD = (1.0, 1.0, 1.0)
TOTAL_AT = 2.0
EARLY_AT = 2.2
AGG_AT = 2.0
FIRST_AT = 3.0
CLOSE_AT = 4


def run_loop(low, high, body):
    if high - low <= 4:
        for index in range(low, high):
            body(index)
    else:

        def step(index, carry):
            body(index)
            return carry

        lax.fori_loop(low, high, step, 0)


def diagonal(count):
    shape = (count, count)
    return lax.broadcasted_iota(jnp.int32, shape, 0) == lax.broadcasted_iota(jnp.int32, shape, 1)


def to_column(row):
    return jnp.sum(jnp.where(diagonal(row.shape[1]), row, 0.0), axis=1, keepdims=True)


def to_row(column):
    return jnp.sum(jnp.where(diagonal(column.shape[0]), column, 0.0), axis=0, keepdims=True)


def pair_tile(pair, part_cols, half, span):
    return jnp.minimum((pair * part_cols) // LANES, (half - span) // LANES)


def make_sends(n_half, n_first, n_pieces):
    first, last = range(n_first), range(n_first, n_pieces)
    near = [("m", k, p) for p in first for k in range(1, n_half)]
    near += [(kind, k, p) for p in last for k in range(1, n_half) for kind in ("m", "x")]
    far = [("m", n_half + k, p) for p in first for k in range(n_half)]
    late = [("m", n_half + k, p) for p in last for k in range(n_half)]
    count = len(first) * (n_half - 1)
    return near[:count] + far + near[count:] + late


def make_events(n_half, n_first, n_pieces):
    first, last = range(n_first), range(n_first, n_pieces)
    sends = make_sends(n_half, n_first, n_pieces)
    own = [("m", 0, p) for p in first]
    fill = [(kind, 0, p) for p in last for kind in ("m", "x")]
    early = len(fill) // 2
    return own + fill[:early] + sends[: n_half - 1] + fill[early:] + sends[n_half - 1 :]


def make_steps(events, n_half, n_first, n_pieces):
    number = {event: index for index, event in enumerate(events)}
    count = len(events)
    steps = [(index, "relay", event) for index, event in enumerate(events)]
    for index, event in enumerate(events[LAG:]):
        at = index if index + LAG < count - len(AHEAD) else index - AHEAD[index + LAG - count]
        steps.append((at + 0.1, "take", event))
    totals = []
    for p in range(n_pieces):
        kinds = ("m",) if p < n_first else ("m", "x")
        need = max(number[(kind, k, p)] for kind in kinds for k in range(n_half))
        steps.append((need + 0.5, "near", p))
        total = need + 0.5 + (TOTAL_AT if p == n_pieces - 1 else EARLY_AT)
        if p < n_first:
            need = max(number[("m", n_half + k, p)] for k in range(n_half))
            steps.append((need + 0.6, "far", p))
            steps.append((need + 0.6 + AGG_AT, "agg", p))
            total = max(total, need + 0.6 + AGG_AT + FIRST_AT)
        totals.append(total)
    totals[-1] = max(totals[-1], max(totals) + 0.01)
    steps += [(total, "total", p) for p, total in enumerate(totals)]
    steps.sort(key=lambda step: step[0])
    return [step[1:] for step in steps]


def kernel(
    n_lib,
    n_ptl,
    span,
    n_first,
    part_hbm,
    shift_hbm,
    table_hbm,
    refs_hbm,
    noise_hbm,
    class_hbm,
    gath,
    final,
    small_ref,
    shift_ref,
    table_ref,
    noise_ref,
    class_ref,
    part_ref,
    shifted,
    extra,
    refbuf,
    weighted,
    noise_row,
    near_part,
    near_recv,
    far_part,
    far_recv,
    agg_recv,
    share_out,
    share_in,
    factor,
    lines,
    raw,
    brief,
    post,
    in_sem,
    part_sem,
    ref_sem,
    own_sem,
    z_send,
    z_recv,
    x_send,
    x_recv,
    c_send,
    c_recv,
    n_send,
    n_recv,
    f_send,
    f_recv,
    g_send,
    g_recv,
    t_send,
    t_recv,
    p_send,
    p_recv,
    b_send,
    b_recv,
):
    lib = lax.axis_index("lib")
    ptl = lax.axis_index("ptl")
    n_x = n_lib // 2
    n_half = n_ptl // 2
    x, core = lib // 2, lib % 2
    mate = 2 * x + 1 - core
    local = lax.rem(ptl, n_half)
    side = ptl // n_half
    n_pieces, _, width = part_ref.shape
    half = width // 2
    part_cols = width // n_ptl
    n_last = n_pieces - n_first
    group = n_lib * ROWS
    tiles = span // LANES

    def near_to(k):
        return side * n_half + lax.rem(local + k, n_half)

    def near_from(k):
        return side * n_half + lax.rem(local + n_half - k, n_half)

    def far_to(k):
        return (1 - side) * n_half + lax.rem(local + k, n_half)

    def far_from(k):
        return (1 - side) * n_half + lax.rem(local + n_half - k, n_half)

    in_copies = [
        pltpu.make_async_copy(source, target, in_sem.at[i])
        for i, (source, target) in enumerate(
            (
                (shift_hbm, shift_ref),
                (table_hbm, table_ref),
                (noise_hbm, noise_ref),
                (class_hbm, class_ref),
            )
        )
    ]
    for copy in in_copies:
        copy.start()
    part_copies = [
        pltpu.make_async_copy(part_hbm.at[pl.ds(p * ROWS, ROWS)], part_ref.at[p], part_sem.at[p])
        for p in range(n_pieces)
    ]
    for copy in part_copies:
        copy.start()
    barrier = pltpu.get_barrier_semaphore()

    def greet_ptl(step):
        pl.semaphore_signal(barrier, inc=1, device_id={"ptl": lax.rem(ptl + step, n_ptl)})

    def greet_lib(step):
        pl.semaphore_signal(barrier, inc=1, device_id={"lib": lax.rem(lib + step, n_lib)})

    run_loop(1, n_ptl, greet_ptl)
    run_loop(1, n_lib, greet_lib)

    own_tile = pair_tile(local, part_cols, half, span)

    def chunk_at(tile):
        return pl.ds(pl.multiple_of(tile * LANES, LANES), span)

    side_tiles = (half // LANES) * side
    ref_copies = [
        pltpu.make_async_copy(
            refs_hbm.at[:, chunk_at(own_tile + (side_tiles if b == 0 else half // LANES - side_tiles))],
            refbuf.at[b],
            ref_sem.at[b],
        )
        for b in range(2)
    ]

    in_copies[0].wait()
    in_copies[1].wait()
    ids = to_column(shift_ref[...].astype(jnp.float32)).astype(jnp.int32)
    step_y = (ids >= 3).astype(jnp.int32) + (ids >= 6).astype(jnp.int32)
    step_x = (ids - 3 * step_y - 1).astype(jnp.float32)
    step_y = (step_y - 1).astype(jnp.float32)
    cos_x = jnp.where(step_x == 0.0, 1.0, table_ref[0:1, 0:LANES])
    sin_x = step_x * table_ref[1:2, 0:LANES]

    def shift(k, p):
        first = pair_tile(lax.rem(local + k, n_half), part_cols, half, span)
        rows = slice(p * ROWS, (p + 1) * ROWS)
        zero_y, turn_y = step_y[rows] == 0.0, step_y[rows]
        cx, sx = cos_x[rows], sin_x[rows]
        for tile in range(tiles):
            at = pl.multiple_of((first + tile) * LANES, LANES)
            lo, hi = pl.ds(at, LANES), pl.ds(pl.multiple_of(at + half, LANES), LANES)
            cos_y = jnp.where(zero_y, 1.0, table_ref[2:3, lo])
            sin_y = turn_y * table_ref[3:4, lo]
            cosine = cx * cos_y - sx * sin_y
            sine = sx * cos_y + cx * sin_y
            real = part_ref[p, :, lo].astype(jnp.float32)
            imag = part_ref[p, :, hi].astype(jnp.float32)
            to = slice(tile * LANES, (tile + 1) * LANES)
            shifted[k, 0, p, :, to] = (real * cosine + imag * sine).astype(jnp.bfloat16)
            shifted[k, 1, p, :, to] = (imag * cosine - real * sine).astype(jnp.bfloat16)

    events = make_events(n_half, n_first, n_pieces)
    number = {event: index for index, event in enumerate(events)}

    def place(event, source):
        kind, slot, p = event
        return gath.at[p, slot, source] if kind == "m" else extra.at[p - n_first, slot, source]

    def which(event):
        kind, slot, _ = event
        return side if (kind == "m") == (slot < n_half) else 1 - side

    def z_copy(event, back=False):
        kind, slot, p = event
        k = slot % n_half
        target = (near_from(k) if back else near_to(k)) if slot < n_half else (
            far_from(k) if back else far_to(k)
        )
        return pltpu.make_async_remote_copy(
            src_ref=shifted.at[k, which(event), p],
            dst_ref=place(event, lib),
            send_sem=z_send.at[number[event]],
            recv_sem=z_recv.at[number[event]],
            device_id={"ptl": target},
        )

    def x_source(d):
        return lax.rem(x - d + n_x, n_x) * 2 + core

    def lib_copy(event, d, source, send, recv, to):
        here = source is lib and event[1] == 0
        return pltpu.make_async_remote_copy(
            src_ref=shifted.at[0, which(event), event[2]] if here else place(event, source),
            dst_ref=place(event, source),
            send_sem=send.at[number[event], d],
            recv_sem=recv.at[number[event], d],
            device_id={"lib": to},
        )

    def x_copy(event, d):
        return lib_copy(event, d - 1, lib, x_send, x_recv, lax.rem(x + d, n_x) * 2 + core)

    def x_arrival(event, d):
        return lib_copy(event, d - 1, x_source(d), x_send, x_recv, x_source(d))

    def core_copy(event, d):
        return lib_copy(event, d, lib if isinstance(d, int) and d == 0 else x_source(d), c_send, c_recv, mate)

    def core_arrival(event, d):
        return lib_copy(event, d, x_source(d) + 1 - 2 * core, c_send, c_recv, mate)

    def spread(event):
        run_loop(1, n_x, lambda d: x_copy(event, d).start())
        core_copy(event, 0).start()

    def take(event):
        if event[1]:
            z_copy(event, True).wait_recv()
        spread(event)

    def relay(event):
        def forward(d):
            x_arrival(event, d).wait_recv()
            core_copy(event, d).start()

        run_loop(1, n_x, forward)

    def settle(event):
        run_loop(0, n_x, lambda d: core_arrival(event, d).wait_recv())

    own_copies = {}

    def keep(event):
        own_copies[event] = pltpu.make_async_copy(
            shifted.at[0, which(event), event[2]], place(event, lib), own_sem.at[number[event]]
        )
        own_copies[event].start()

    ready, queue = set(), make_sends(n_half, n_first, n_pieces)
    taken = events[:LAG]

    def issue():
        while queue and (queue[0][1] % n_half, queue[0][2]) in ready:
            z_copy(queue.pop(0)).start()
        while taken and (0, taken[0][2]) in ready:
            take(taken.pop(0))

    for p in range(n_pieces):
        part_copies[p].wait()
        for k in range(n_half):
            shift(k, p)
            if not ready:
                pl.semaphore_wait(barrier, n_ptl - 1 + n_lib - 1)
            ready.add((k, p))
            issue()
            if len(ready) == 1:
                for copy in ref_copies:
                    copy.start()
        keep(("m", 0, p))
        if p >= n_first:
            keep(("x", 0, p))

    in_copies[2].wait()
    in_copies[3].wait()
    for tile in range(half // LANES):
        noise_row[:, tile * LANES : (tile + 1) * LANES] = noise_ref[tile : tile + 1, :]
    offset = local * part_cols - own_tile * LANES
    spot = lax.broadcasted_iota(jnp.int32, (1, span), 1)
    inside = (spot >= offset) & (spot < offset + part_cols)
    noise = jnp.where(inside, noise_row[:, chunk_at(own_tile)], 0.0)
    norms = []
    for b in range(2):
        ref_copies[b].wait()
        widened = refbuf[b].astype(jnp.float32)
        scaled = widened * noise
        weighted[b] = scaled.astype(jnp.bfloat16)
        norms.append(to_row(0.5 * jnp.sum(widened * scaled, axis=1, keepdims=True)))

    def dot(images, b):
        return lax.dot_general(
            images, weighted[b], (((1,), (1,)), ((), ())), preferred_element_type=jnp.float32
        )

    def images_of(ref, low):
        return ref[low : low + n_half].reshape(n_half * group, span)

    def near_copy(p, k, back=False):
        return pltpu.make_async_remote_copy(
            src_ref=near_part.at[p, k],
            dst_ref=near_recv.at[p, k - 1],
            send_sem=n_send.at[p, k - 1],
            recv_sem=n_recv.at[p, k - 1],
            device_id={"ptl": near_to(k) if back else near_from(k)},
        )

    def far_copy(p, k, back=False):
        return pltpu.make_async_remote_copy(
            src_ref=far_part.at[p, k],
            dst_ref=far_recv.at[p, k - 1],
            send_sem=f_send.at[p, k - 1],
            recv_sem=f_recv.at[p, k - 1],
            device_id={"ptl": near_to(k) if back else near_from(k)},
        )

    def agg_copy(p):
        return pltpu.make_async_remote_copy(
            src_ref=far_part.at[p, 0],
            dst_ref=agg_recv.at[p],
            send_sem=g_send.at[p],
            recv_sem=g_recv.at[p],
            device_id={"ptl": far_to(0)},
        )

    def share_copy(d):
        to = lax.rem(lib + d, n_lib)
        return pltpu.make_async_remote_copy(
            src_ref=share_out.at[to],
            dst_ref=share_in.at[d - 1],
            send_sem=t_send.at[d - 1],
            recv_sem=t_recv.at[d - 1],
            device_id={"lib": to},
        )

    def post_copy(p, slot, back=False):
        k = slot % n_half
        if slot < n_half:
            target = near_from(k) if back else near_to(k)
        else:
            target = far_from(k) if back else far_to(k)
        return pltpu.make_async_remote_copy(
            src_ref=post.at[p, 0],
            dst_ref=post.at[p, slot],
            send_sem=p_send.at[p, slot - 1],
            recv_sem=p_recv.at[p, slot - 1],
            device_id={"ptl": target},
        )

    def brief_copy(slot, d, back=False):
        k = slot % n_half
        if slot < n_half:
            target = near_from(k) if back else near_to(k)
        else:
            target = far_from(k) if back else far_to(k)
        return pltpu.make_async_remote_copy(
            src_ref=brief.at[0, 0],
            dst_ref=brief.at[slot, d],
            send_sem=b_send.at[slot, d],
            recv_sem=b_recv.at[slot, d],
            device_id={"ptl": target, "lib": lax.rem(lib + (n_lib - d if back else d), n_lib)},
        )

    onehot = (
        class_ref[...] == lax.broadcasted_iota(jnp.int32, (CLASSES, class_ref.shape[1]), 0)
    ).astype(jnp.bfloat16)

    final_piece = n_pieces - 1

    def step_near(p):
        kinds = ("m",) if p < n_first else ("m", "x")
        for kind in kinds:
            own_copies[(kind, 0, p)].wait()
            for k in range(n_half):
                settle((kind, k, p))
        scores = dot(images_of(gath.at[p], 0), 0) - norms[0]
        if p >= n_first:
            scores = scores + (dot(images_of(extra.at[p - n_first], 0), 1) - norms[1])
        near_part[p] = scores.reshape(n_half, group, -1)
        for k in range(1, n_half):
            near_copy(p, k).start()

    def step_far(p):
        for k in range(n_half):
            settle(("m", n_half + k, p))
        scores = dot(images_of(gath.at[p], n_half), 0) - norms[0]
        far_part[p] = scores.reshape(n_half, group, -1)
        for k in range(1, n_half):
            far_copy(p, k).start()

    def step_agg(p):
        for k in range(1, n_half):
            far_copy(p, k, True).wait_recv()
            far_copy(p, k).wait_send()
            far_part[p, 0] = far_part[p, 0] + far_recv[p, k - 1]
        agg_copy(p).start()

    def step_total(p):
        scores = near_part[p, 0]
        for k in range(1, n_half):
            near_copy(p, k, True).wait_recv()
            near_copy(p, k).wait_send()
            scores = scores + near_recv[p, k - 1]
        if p < n_first:
            agg_copy(p).wait_recv()
            agg_copy(p).wait_send()
            scores = scores + agg_recv[p]
        scores = scores.T
        peak = jnp.max(scores, axis=0, keepdims=True)
        weights = jnp.exp(scores - peak)
        mass = jnp.sum(weights, axis=0, keepdims=True)
        wide = slice(p * group, (p + 1) * group)
        brief[0, 0, 0:1, wide] = peak
        brief[0, 0, 1:2, wide] = mass
        post[p, 0] = weights.T.astype(jnp.bfloat16)
        for slot in reversed(range(1, n_ptl)):
            post_copy(p, slot).start()
        if p == final_piece:
            for slot in reversed(range(n_ptl)):
                run_loop(0 if slot else 1, n_lib, lambda d: brief_copy(slot, d).start())
        shares = jnp.dot(onehot, weights.astype(jnp.bfloat16), preferred_element_type=jnp.float32)
        mine = slice(p * ROWS, (p + 1) * ROWS)
        for l in range(n_lib):
            share_out[l, :, mine] = shares[:, l * ROWS : (l + 1) * ROWS]
        if p == final_piece:
            run_loop(1, n_lib, lambda d: share_copy(d).start())

    def total_of(slot):
        top = brief[slot, 0, 0:1]
        for d in range(1, n_lib):
            top = jnp.maximum(top, brief[slot, d, 0:1])
        total = jnp.zeros_like(top)
        for d in range(n_lib):
            total = total + brief[slot, d, 1:2] * jnp.exp(brief[slot, d, 0:1] - top)
        return top + jnp.log(total)

    def pick(values, p):
        low = p * group
        mine = values[:, low : low + ROWS]
        for l in range(1, n_lib):
            at = low + l * ROWS
            mine = jnp.where(lib == l, values[:, at : at + ROWS], mine)
        return mine

    def step_post():
        run_loop(1, n_lib, lambda d: brief_copy(0, d, True).wait_recv())
        evidence = total_of(0)
        for d in range(n_lib):
            lines[d : d + 1] = jnp.exp(brief[0, d, 0:1] - evidence)
        lines[n_lib : n_lib + 1] = evidence
        for p in range(n_pieces):
            mine = slice(p * ROWS, (p + 1) * ROWS)
            factor[:, mine] = pick(lines[...], p)
        small_ref[0:1] = factor[n_lib : n_lib + 1]
        share = share_out[lib] * factor[0:1]
        for d in range(1, n_lib):
            share_copy(d).wait_recv()
            share = share + share_in[d - 1] * factor[d : d + 1]
        small_ref[8 : 8 + CLASSES] = share

    def places(p, slot):
        low = (p * n_ptl + slot) * group
        return slice(low, low + 2 * group)

    def step_turn(p):
        for slot in range(1, n_ptl):
            post_copy(p, slot, True).wait_recv()
            if p < final_piece:
                post_copy(p, slot).wait_send()
        for slot in range(0, n_ptl, 2):
            pair = post[p, slot : slot + 2].reshape(2 * group, -1)
            raw[:, places(p, slot)] = pair.astype(jnp.float32).T

    def step_scale():
        for slot in range(1, n_ptl):
            run_loop(0, n_lib, lambda d: brief_copy(slot, d, True).wait_recv())
        scales = [jnp.exp(brief[slot, 0, 0:1] - total_of(slot)) for slot in range(n_ptl)]
        for p in range(n_pieces):
            wide = slice(p * group, (p + 1) * group)
            for slot in range(0, n_ptl, 2):
                row = jnp.concatenate([scales[slot][:, wide], scales[slot + 1][:, wide]], axis=1)
                at = places(p, slot)
                final[:, at] = (raw[:, at] * row).astype(jnp.bfloat16)

    acts = {
        "relay": relay,
        "take": take,
        "near": step_near,
        "far": step_far,
        "agg": step_agg,
        "total": step_total,
    }
    def close(event):
        run_loop(1, n_x, lambda d: x_copy(event, d).wait_send())
        run_loop(0, n_x, lambda d: core_copy(event, d).wait_send())

    sends = make_sends(n_half, n_first, n_pieces)
    open_events, open_sends = list(events), list(sends)
    for name, subject in make_steps(events, n_half, n_first, n_pieces):
        acts[name](subject)
        if name == "relay" and number[subject] >= CLOSE_AT:
            close(open_events.pop(0))
            for event in open_sends[:1]:
                z_copy(open_sends.pop(0)).wait_send()

    for p in range(n_pieces - 1):
        step_turn(p)
    step_post()
    step_turn(n_pieces - 1)
    step_scale()
    for event in events:
        if event[1] >= n_half and event[2] >= n_first:
            settle(event)

    run_loop(1, n_lib, lambda d: share_copy(d).wait_send())
    for slot in range(n_ptl):
        run_loop(0 if slot else 1, n_lib, lambda d: brief_copy(slot, d).wait_send())
    for event in open_sends:
        z_copy(event).wait_send()
    for event in open_events:
        close(event)
    for slot in range(1, n_ptl):
        post_copy(final_piece, slot).wait_send()


def finish(n_ptl, blocks, images, weights, small, sums, evid, share, total, buffer, own, sem, small_sem):
    part_cols = sums.shape[0]
    span = images.shape[1]
    half = n_ptl * part_cols // 2
    z = lax.axis_index("ptl")
    pair = lax.rem(z, n_ptl // 2)
    offset = pair * part_cols - pair_tile(pair, part_cols, half, span) * LANES
    slack = span - part_cols
    block = span // blocks
    copies = [
        pltpu.make_async_copy(small.at[pl.ds(0, 1)], evid, small_sem.at[0]),
        pltpu.make_async_copy(small.at[pl.ds(8, CLASSES)], share, small_sem.at[1]),
    ]
    for copy in copies:
        copy.start()
    ones = jnp.ones((8, weights.shape[1]), jnp.bfloat16)
    totals = lax.dot_general(
        ones, weights[...], (((1,), (1,)), ((), ())), preferred_element_type=jnp.float32
    )
    count = total.shape[1]
    own_total = totals[0:1, 0:count]
    for y in range(1, n_ptl):
        own_total = jnp.where(z == y, totals[0:1, y * count : (y + 1) * count], own_total)
    own[...] = own_total
    copies.append(pltpu.make_async_copy(own, total, small_sem.at[2]))
    copies[-1].start()
    for b in range(blocks):
        cols = slice(b * block, (b + 1) * block)
        buffer[cols] = jnp.dot(
            weights[...], images[:, cols], preferred_element_type=jnp.float32
        ).T
        low = b * block - slack if b else 0
        size = (b + 1) * block - slack - low
        copies.append(
            pltpu.make_async_copy(
                buffer.at[pl.ds(pl.multiple_of(offset + low, 8), size)],
                sums.at[pl.ds(low, size)],
                sem.at[b],
            )
        )
        copies[-1].start()
    for copy in copies:
        copy.wait()


def trig_table(half):
    index = np.arange(half)
    angle_x = (index % 64) * (2.0 * math.pi / 128.0)
    angle_y = (index // 64) * (2.0 * math.pi / 128.0)
    table = np.zeros((8, half), np.float32)
    table[0], table[1] = np.cos(angle_x), np.sin(angle_x)
    table[2], table[3] = np.cos(angle_y), np.sin(angle_y)
    return table


def on_device(n_lib, n_ptl, particles, shifts, references, inv_noise, proj_class):
    rows, width = particles.shape
    projections = references.shape[0]
    half = width // 2
    part_cols = width // n_ptl
    n_half = n_ptl // 2
    n_x = n_lib // 2
    cover = 0
    for pair in range(n_half):
        cover = max(cover, -(-(pair * part_cols % LANES + part_cols) // LANES))
    span = min(cover * LANES, half)
    n_pieces = rows // ROWS
    n_first = 1
    n_last = n_pieces - n_first
    group = n_lib * ROWS
    own_total = projections // n_ptl
    n_events = len(make_events(n_half, n_first, n_pieces))
    blocks = 5 if (span // LANES) % 5 == 0 else 1
    vmem = pl.BlockSpec(memory_space=pltpu.VMEM)
    far = pl.BlockSpec(memory_space=pltpu.HBM)
    dma = pltpu.SemaphoreType.DMA
    score = (group, projections)
    held_bytes = 2 * n_pieces * n_ptl * group * (span + projections)
    mib = 1024 * 1024
    vmem_limit = (55 - held_bytes // mib) * mib
    images, weights, small = pl.pallas_call(
        functools.partial(kernel, n_lib, n_ptl, span, n_first),
        out_shape=(
            pltpu.VMEM((n_pieces, n_ptl, n_lib, ROWS, span), jnp.bfloat16),
            pltpu.VMEM((projections, n_pieces * n_ptl * group), jnp.bfloat16),
            pltpu.VMEM((8 + CLASSES, rows), jnp.float32),
        ),
        in_specs=[far] * 6,
        out_specs=(vmem, vmem, vmem),
        scratch_shapes=[
            pltpu.VMEM((1, rows), jnp.int32),
            pltpu.VMEM((8, half), jnp.float32),
            pltpu.VMEM((half // LANES, LANES), jnp.float32),
            pltpu.VMEM((1, projections), jnp.int32),
            pltpu.VMEM((n_pieces, ROWS, width), jnp.bfloat16),
            pltpu.VMEM((n_half, 2, n_pieces, ROWS, span), jnp.bfloat16),
            pltpu.VMEM((n_last, n_half, n_lib, ROWS, span), jnp.bfloat16),
            pltpu.VMEM((2, projections, span), jnp.bfloat16),
            pltpu.VMEM((2, projections, span), jnp.bfloat16),
            pltpu.VMEM((1, half), jnp.float32),
            pltpu.VMEM((n_pieces, n_half, *score), jnp.float32),
            pltpu.VMEM((n_pieces, n_half - 1, *score), jnp.float32),
            pltpu.VMEM((n_first, n_half, *score), jnp.float32),
            pltpu.VMEM((n_first, n_half - 1, *score), jnp.float32),
            pltpu.VMEM((n_first, *score), jnp.float32),
            pltpu.VMEM((n_lib, CLASSES, rows), jnp.float32),
            pltpu.VMEM((n_lib - 1, CLASSES, rows), jnp.float32),
            pltpu.VMEM((n_lib + 1, rows), jnp.float32),
            pltpu.VMEM((n_lib + 1, n_pieces * group), jnp.float32),
            pltpu.VMEM((projections, n_pieces * n_ptl * group), jnp.float32),
            pltpu.VMEM((n_ptl, n_lib, 2, n_pieces * group), jnp.float32),
            pltpu.VMEM((n_pieces, n_ptl, group, projections), jnp.bfloat16),
            dma((4,)),
            dma((n_pieces,)),
            dma((2,)),
            dma((n_events,)),
            dma((n_events,)),
            dma((n_events,)),
            dma((n_events, n_x - 1)),
            dma((n_events, n_x - 1)),
            dma((n_events, n_x)),
            dma((n_events, n_x)),
            dma((n_pieces, n_half - 1)),
            dma((n_pieces, n_half - 1)),
            dma((n_first, n_half - 1)),
            dma((n_first, n_half - 1)),
            dma((n_first,)),
            dma((n_first,)),
            dma((n_lib - 1,)),
            dma((n_lib - 1,)),
            dma((n_pieces, n_ptl - 1)),
            dma((n_pieces, n_ptl - 1)),
            dma((n_ptl, n_lib)),
            dma((n_ptl, n_lib)),
        ],
        compiler_params=pltpu.CompilerParams(
            collective_id=0, has_side_effects=True, vmem_limit_bytes=vmem_limit
        ),
    )(
        particles,
        shifts[None, :],
        trig_table(half),
        references,
        inv_noise.reshape(-1, LANES),
        proj_class[None, :],
    )
    total_rows = n_pieces * n_ptl * group
    sums, evidence, share, total = pl.pallas_call(
        functools.partial(finish, n_ptl, blocks),
        out_shape=(
            pltpu.HBM((part_cols, projections), jnp.float32),
            pltpu.HBM((1, rows), jnp.float32),
            pltpu.HBM((CLASSES, rows), jnp.float32),
            pltpu.HBM((1, own_total), jnp.float32),
        ),
        in_specs=[vmem, vmem, vmem],
        out_specs=(far, far, far, far),
        scratch_shapes=[
            pltpu.VMEM((span, projections), jnp.float32),
            pltpu.VMEM((1, own_total), jnp.float32),
            dma((blocks,)),
            dma((3,)),
        ],
        compiler_params=pltpu.CompilerParams(vmem_limit_bytes=24 * mib),
    )(images.reshape(total_rows, span), weights, small)
    return evidence[0], share.T, sums.T, total[0]


def solution(mesh):
    in_specs = (
        P(("grp", "lib", "ptl"), None),
        P(("grp", "lib", "ptl")),
        P(("grp", "lib"), None),
        P("grp"),
        P("lib"),
    )
    out_specs = (
        P(("grp", "lib", "ptl")),
        P(("grp", "lib", "ptl"), None),
        P(("grp", "lib"), "ptl"),
        P(("grp", "lib", "ptl")),
    )
    return jax.shard_map(
        functools.partial(on_device, mesh.shape["lib"], mesh.shape["ptl"]),
        mesh=mesh,
        in_specs=in_specs,
        out_specs=out_specs,
        check_vma=False,
    )
```
